32 devices in a mesh: expert: 8 (over y, x, core), weight: 4 (over z).
Axes of the slice: x: 2, y: 2, z: 4, core: 2. Of those that a mesh axis runs over, the one named last changes fastest.
Arguments:
- block_input: bfloat16 [4096, 2048], P('expert'), may hold values from -6 to 6
- out_grad: float32 [4096, 2048], P('expert'), may hold values from -6 to 6
- norm_one: float32 [2048], replicated, may hold values from 0.5 to 1.5
- query_weight: bfloat16 [2048, 2048], P(None, 'weight'), may hold values from -0.125 to 0.125
- key_weight: bfloat16 [2048, 2048], P(None, 'weight'), may hold values from -0.125 to 0.125
- value_weight: bfloat16 [2048, 2048], P(None, 'weight'), may hold values from -0.125 to 0.125
- query_gain: float32 [16, 128], P('weight'), may hold values from 0.5 to 1.5
- key_gain: float32 [16, 128], P('weight'), may hold values from 0.5 to 1.5
- output_weight: bfloat16 [2048, 2048], P('weight'), may hold values from -1 to 1
- norm_two: float32 [2048], replicated, may hold values from 0.5 to 1.5
- router_weight: bfloat16 [2048, 64], replicated, may hold values from -0.125 to 0.125
- gate_weight: bfloat16 [64, 2048, 1024], P('expert', None, 'weight'), may hold values from -0.125 to 0.125
- up_weight: bfloat16 [64, 2048, 1024], P('expert', None, 'weight'), may hold values from -0.125 to 0.125
- down_weight: bfloat16 [64, 1024, 2048], P('expert', 'weight'), may hold values from -8 to 8
- segment_ids: int32 [8, 512], P('expert'), may hold values from 0 to 2, never falling along the last dimension, each value on 1 to 256 neighbouring positions
- expert_routes: int32 [4096, 8], P('expert'), may hold values from 0 to 63, as said below
- expert_slots: int32 [4096, 8], P('expert'), may hold values from 0 to 96, as said below
Outputs:
- block_output: float32 [4096, 2048], P('expert', 'weight')
- input_grad: float32 [4096, 2048], P(('expert', 'weight'))
- norm_one_grad: float32 [2048], P('expert')
- query_weight_grad: float32 [2048, 2048], P('expert', 'weight')
- key_weight_grad: float32 [2048, 2048], P('expert', 'weight')
- value_weight_grad: float32 [2048, 2048], P('expert', 'weight')
- query_gain_grad: float32 [16, 128], P('weight', 'expert')
- key_gain_grad: float32 [16, 128], P('weight', 'expert')
- output_weight_grad: float32 [2048, 2048], P('weight', 'expert')
- norm_two_grad: float32 [2048], P('expert')
- router_grad: float32 [2048, 64], P('expert', 'weight')
- gate_grad: float32 [64, 2048, 1024], P('expert', None, 'weight')
- up_grad: float32 [64, 2048, 1024], P('expert', None, 'weight')
- down_grad: float32 [64, 1024, 2048], P('expert', 'weight')
The draws below stay inside these ranges and needn't reach their ends.
Inputs may be any that keep to these rules, and one draw needn't show every extreme that they name: `expert_routes`: each row names 8 different experts. expert_slots[t, k] counts the earlier choices of the same expert among the tokens of t's sequence (earlier tokens, or the same token with smaller k) when that count is under 96, and equals 96 (the choice is dropped) otherwise; in every sequence some expert is chosen more than 96 times.
All inputs are finite; a program needn't handle non-finite values.
Results may differ from the reference program's by a relative error of at most 0.02.
Values may be sent and summed in bfloat16 or wider, within the bound.
No kernel may reach another device: no remote copies, remote signals or barrier semaphores. Data moves between devices by JAX's collectives and lax.ppermute only.
A program may use at most 448 MiB of HBM per device.

```python
import math
import jax
import jax.numpy as jnp
import numpy as np
from jax import lax

D = 2048
HEADS = 16
HD = 128
FF = 1024
EXPERTS = 64
TOP = 8
TOK_DEV = 512
DOCS = 3
SEQS = 8
TOKENS = 4096
CAP = 96
N_WEIGHT = 4


def route_table(key):
    route_key = jax.random.fold_in(key, 4711)
    level_key, noise_key, hot_key = jax.random.split(route_key, 3)
    levels = jax.random.randint(level_key, (EXPERTS,), 0, 3)
    noise_bits = jax.random.randint(noise_key, (TOKENS, EXPERTS), 0, 2 ** 20)
    block_total = TOKENS // TOK_DEV
    hottest = jax.random.randint(hot_key, (block_total,), 0, EXPERTS)
    row_ids = jnp.arange(TOKENS)
    columns = jnp.arange(EXPERTS)
    forced = (row_ids % TOK_DEV <= CAP)[:, None] & (columns[None, :] == hottest[row_ids // TOK_DEV][:, None])
    ranking = (noise_bits + levels[None, :] * 2 ** 17 + forced.astype(jnp.int32) * 2 ** 22) * EXPERTS + columns[None, :]
    top_values, routes = lax.top_k(ranking, TOP)
    chosen = (routes[:, :, None] == columns[None, None, :]).astype(jnp.int32)
    chosen = chosen.reshape(block_total, TOK_DEV * TOP, EXPERTS)
    earlier = jnp.cumsum(chosen, axis=1) - chosen
    slot_values = jnp.sum(earlier * chosen, axis=-1).reshape(TOKENS, TOP)
    return (routes.astype(jnp.int32), jnp.minimum(slot_values, CAP).astype(jnp.int32))


def draw_expert_routes(key, part):
    return route_table(key)[0]


def draw_expert_slots(key, part):
    return route_table(key)[1]


def steps_of(own_key, extent, cuts, least, top_value):
    loudness, own = 1.0, jax.random.fold_in(own_key, 6)
    for axis_at, parts in cuts:
        draws = jnp.exp(jax.random.uniform(jax.random.fold_in(own, axis_at), (parts,), jnp.float32, least / len(cuts), top_value / len(cuts)))
        loudness = loudness * jnp.repeat(draws, extent[axis_at] // parts).reshape([-1 if axis == axis_at else 1 for axis in range(len(extent))])
    return loudness


def length_profile(amount, total, most, lean):
    loads = [(1 << 20) // math.isqrt(rank ** lean) + 1 for rank in range(2, amount + 1)]
    spare, given = total - most - (amount - 1), [1] * (amount - 1)
    while spare > 0:
        free = [i for i in range(amount - 1) if given[i] < most]
        whole, left = sum([loads[i] for i in free]), spare
        for i in free:
            more = min(most - given[i], max(1, left * loads[i] // whole), spare)
            given[i] = given[i] + more
            spare = spare - more
    return np.array([most] + given)


def ragged_sizes(own_key, amount, total, limit, slope):
    if amount == 2:
        one = jax.random.randint(own_key, (), max(1, total - limit), min(limit, total - 1) + 1)
        return jnp.stack([one, total - one])
    sizes = jnp.asarray(length_profile(amount, total, limit, slope), jnp.int32)
    couples = (amount - 1) // 2
    donor, receiver = sizes[1:1 + 2 * couples:2], sizes[2:2 + 2 * couples:2]
    slack = jnp.minimum(donor - 1, limit - receiver)
    shifted = jax.random.randint(jax.random.fold_in(own_key, 1), (couples,), 0, 1 << 20) % (slack + 1)
    sizes = sizes.at[1:1 + 2 * couples:2].set(donor - shifted).at[2:2 + 2 * couples:2].set(receiver + shifted)
    return sizes[jax.random.permutation(jax.random.fold_in(own_key, 2), amount)]


def bell_draw(own_key, shape, width, reach, cuts=(), kind=jnp.bfloat16):
    entries = jax.random.normal(own_key, shape, jnp.float32) * width
    if len(cuts) > 0:
        entries = steps_of(own_key, shape, cuts, -0.22, 0.18) * entries
    return jnp.clip(entries, min=-reach, max=reach).astype(kind)


def setup_inputs(seed: int = 0) -> dict:
    key_of = jax.random.split(jax.random.key(seed), 18)
    block_input = bell_draw(key_of[0], (TOKENS, D), 1.0, 6.0, ((0, 8),))
    out_grad = bell_draw(key_of[1], (TOKENS, D), 1.0, 6.0, ((0, 8),), jnp.float32)
    norm_one = jnp.clip(1.0 + 0.1 * jax.random.normal(key_of[2], (D,), jnp.float32), 0.5, 1.5)
    query_weight = bell_draw(key_of[3], (D, D), D ** -0.5, 0.125, ((1, 4),))
    key_weight = bell_draw(key_of[4], (D, D), D ** -0.5, 0.125, ((1, 4),))
    value_weight = bell_draw(key_of[5], (D, D), D ** -0.5, 0.125, ((1, 4),))
    query_gain = jnp.clip(1.0 + 0.1 * jax.random.normal(key_of[6], (HEADS, HD), jnp.float32), 0.5, 1.5)
    key_gain = jnp.clip(1.0 + 0.1 * jax.random.normal(key_of[7], (HEADS, HD), jnp.float32), 0.5, 1.5)
    output_weight = bell_draw(key_of[8], (D, D), (D // 64) ** -0.5, 1.0, ((0, 4),))
    norm_two = jnp.clip(1.0 + 0.1 * jax.random.normal(key_of[9], (D,), jnp.float32), 0.5, 1.5)
    router_weight = bell_draw(key_of[10], (D, EXPERTS), D ** -0.5, 0.125)
    gate_weight = bell_draw(key_of[11], (EXPERTS, D, FF), D ** -0.5, 0.125, ((0, 8), (2, 4)))
    up_weight = bell_draw(key_of[12], (EXPERTS, D, FF), D ** -0.5, 0.125, ((0, 8), (2, 4)))
    down_weight = bell_draw(key_of[13], (EXPERTS, FF, D), (45.25 * FF ** -0.5), 8.0, ((0, 8), (1, 4)))
    segment_ids = jax.vmap(lambda own: jnp.searchsorted(jnp.cumsum(ragged_sizes(own, DOCS, TOK_DEV, TOK_DEV // 2, 0)), jnp.arange(TOK_DEV), side="right"))(jax.random.split(key_of[14], SEQS)).reshape((SEQS, TOK_DEV)).astype(jnp.int32)
    expert_routes = draw_expert_routes(jax.random.fold_in(key_of[17], 71), 0)
    expert_slots = draw_expert_slots(jax.random.fold_in(key_of[17], 71), 0)
    return dict(block_input=block_input, out_grad=out_grad, norm_one=norm_one, query_weight=query_weight, key_weight=key_weight, value_weight=value_weight, query_gain=query_gain, key_gain=key_gain, output_weight=output_weight, norm_two=norm_two, router_weight=router_weight, gate_weight=gate_weight, up_weight=up_weight, down_weight=down_weight, segment_ids=segment_ids, expert_routes=expert_routes, expert_slots=expert_slots)


@jax.custom_vjp
def low(v):
    return lax.optimization_barrier(v.astype(jnp.bfloat16)).astype(jnp.float32)

@jax.custom_vjp
def low_back(v):
    return v

def low_keep(v):
    return (low(v), None)

def low_pass(kept, grad):
    return (grad,)

def back_keep(v):
    return (v, None)

def back_low(kept, grad):
    return (low(grad),)
low.defvjp(low_keep, low_pass)
low_back.defvjp(back_keep, back_low)
norm_eps = 1e-05
rope_base = 10000.0

def product(left, right):
    return jnp.dot(left, right, precision=lax.Precision.HIGHEST, preferred_element_type=left.dtype)

def rms_scale(values):
    return lax.rsqrt(lax.optimization_barrier(jnp.mean(values * values, axis=-1, keepdims=True)) + norm_eps)

def rope_tables(length, head_width, float_type):
    exponent = jnp.arange(head_width // 2).astype(float_type) * 2.0 / head_width
    inverse = rope_base ** (-exponent)
    angles = jnp.arange(length).astype(float_type)[:, None] * inverse[None, :]
    angles = jnp.concatenate([angles, angles], axis=-1)[:, None, :]
    return (jnp.cos(angles), jnp.sin(angles))

def rotate(values, cosine, sine_table):
    half_width = values.shape[-1] // 2
    turned = jnp.concatenate([-values[..., half_width:], values[..., :half_width]], axis=-1)
    return values * cosine + turned * sine_table

def attend(pieces):
    queries, keys, values, segment_row = pieces
    length = queries.shape[0]
    scores = jnp.einsum('qhd,khd->hqk', queries, keys, precision=lax.Precision.HIGHEST) * HD ** (-0.5)
    scores = low_back(scores)
    positions = jnp.arange(length)
    allowed = (positions[:, None] >= positions[None, :]) & (segment_row[:, None] == segment_row[None, :])
    scores = jnp.where(allowed[None], scores, -1e+30)
    weights_soft = low(jax.nn.softmax(scores, axis=-1))
    return jnp.einsum('hqk,khd->qhd', weights_soft, values, precision=lax.Precision.HIGHEST)

def forward(block_input, norm_one, query_weight, key_weight, value_weight, query_gain, key_gain, output_weight, norm_two, router_weight, gate_weight, up_weight, down_weight, segment_ids, expert_routes, expert_slots):
    float_type = block_input.dtype
    normed_one = low(block_input * rms_scale(block_input) * norm_one)
    query_pre = low_back(product(normed_one, query_weight))
    key_pre = low_back(product(normed_one, key_weight))
    value_all = low(low_back(product(normed_one, value_weight)))
    query_norm = query_pre * rms_scale(query_pre) * query_gain.reshape(-1)
    key_norm = key_pre * rms_scale(key_pre) * key_gain.reshape(-1)
    head_shape = (SEQS, TOK_DEV, HEADS, HD)
    cosine, sine_table = rope_tables(TOK_DEV, HD, float_type)
    query_rot = low(rotate(query_norm.reshape(head_shape), cosine, sine_table))
    key_rot = low(rotate(key_norm.reshape(head_shape), cosine, sine_table))
    attended = lax.map(jax.checkpoint(attend), (query_rot, key_rot, value_all.reshape(head_shape), segment_ids))
    mixed = low(low_back(attended.reshape(TOKENS, D)))
    second = block_input + low_back(product(mixed, output_weight))
    normed_two = low(second * rms_scale(second) * norm_two)
    gate_soft = jax.nn.softmax(low_back(product(normed_two, router_weight)), axis=-1)
    sources = (jnp.arange(TOKENS) // TOK_DEV).astype(jnp.int32)
    token_ids = jnp.broadcast_to(jnp.arange(TOKENS).astype(jnp.int32)[:, None], expert_routes.shape)
    places = jnp.where(expert_slots < CAP, (expert_routes * SEQS + sources[:, None]) * CAP + expert_slots, EXPERTS * SEQS * CAP).astype(jnp.int32)
    table = jnp.full((EXPERTS * SEQS * CAP + 1,), TOKENS, jnp.int32)
    table = table.at[places.reshape(-1)].set(token_ids.reshape(-1).astype(jnp.int32))
    table = table[:-1].reshape(EXPERTS, SEQS * CAP)
    padded_rows = jnp.concatenate([normed_two, jnp.zeros((1, D), float_type)], axis=0)
    padded_gates = jnp.concatenate([gate_soft, jnp.zeros((1, EXPERTS), float_type)], axis=0)
    group_width = FF // N_WEIGHT

    def expert_step(pieces):
        gate_mat, up_mat, down_mat, row_ids, expert_id = pieces
        rows_in = padded_rows[row_ids]
        gate_values = padded_gates[row_ids, expert_id]
        combined = jnp.zeros((row_ids.shape[0], D), float_type)
        for group in range(N_WEIGHT):
            first_col = group * group_width
            expert_in = low_back(rows_in)
            gate_pre = low_back(product(expert_in, gate_mat[:, first_col:first_col + group_width]))
            up_pre = low_back(product(expert_in, up_mat[:, first_col:first_col + group_width]))
            hidden = low(jax.nn.silu(gate_pre) * up_pre)
            combined = combined + low(low_back(product(hidden, down_mat[first_col:first_col + group_width, :])))
        return gate_values[:, None] * combined
    expert_ids = jnp.arange(EXPERTS).astype(jnp.int32)
    outputs = lax.map(jax.checkpoint(expert_step), (gate_weight, up_weight, down_weight, table, expert_ids))
    mixture = jnp.zeros((TOKENS + 1, D), float_type).at[table.reshape(-1)].add(outputs.reshape(-1, D))
    return second + mixture[:TOKENS]

def reference(block_input, out_grad, norm_one, query_weight, key_weight, value_weight, query_gain, key_gain, output_weight, norm_two, router_weight, gate_weight, up_weight, down_weight, segment_ids, expert_routes, expert_slots):
    floats = (block_input.astype(jnp.float32), norm_one.astype(jnp.float32), query_weight.astype(jnp.float32), key_weight.astype(jnp.float32), value_weight.astype(jnp.float32), query_gain.astype(jnp.float32), key_gain.astype(jnp.float32), output_weight.astype(jnp.float32), norm_two.astype(jnp.float32), router_weight.astype(jnp.float32), gate_weight.astype(jnp.float32), up_weight.astype(jnp.float32), down_weight.astype(jnp.float32))

    def apply_block(*weights):
        return forward(*weights, segment_ids, expert_routes, expert_slots)
    block_output, pullback = jax.vjp(apply_block, *floats)
    grads = pullback(out_grad.astype(block_output.dtype))
    return (block_output, grads[0], grads[1], grads[2], grads[3], grads[4], grads[5], grads[6], grads[7], grads[8], grads[9], grads[10], grads[11], grads[12])
```

```python
import jax
import jax.numpy as jnp
from jax import lax
from jax.sharding import PartitionSpec as P

D = 2048
HD = 128
EXPERTS = 64
TOP = 8
CAP = 96
EXTRA = 128
WIDE = D + EXTRA
BF = jnp.bfloat16
F32 = jnp.float32

norm_eps = 1e-05
rope_base = 10000.0


def rms_scale(values):
    return lax.rsqrt(jnp.mean(values * values, axis=-1, keepdims=True) + norm_eps)


def rope_tables(length, head_width):
    exponent = jnp.arange(head_width // 2).astype(F32) * 2.0 / head_width
    inverse = rope_base ** (-exponent)
    angles = jnp.arange(length).astype(F32)[:, None] * inverse[None, :]
    angles = jnp.concatenate([angles, angles], axis=-1)[:, None, :]
    return (jnp.cos(angles), jnp.sin(angles))


def rotate(values, cosine, sine_table):
    half_width = values.shape[-1] // 2
    turned = jnp.concatenate([-values[..., half_width:], values[..., :half_width]], axis=-1)
    return values * cosine + turned * sine_table


def rotate_back(values, cosine, sine_table):
    half_width = values.shape[-1] // 2
    shifted = values * sine_table
    turned = jnp.concatenate([shifted[..., half_width:], -shifted[..., :half_width]], axis=-1)
    return values * cosine + turned


def dot32(left, right):
    return jnp.dot(left, right, preferred_element_type=F32)


def swap(values, distance):
    count = lax.axis_size("expert")
    return lax.ppermute(values, "expert", [(i, i ^ distance) for i in range(count)])


def swap_weight(values, distance):
    count = lax.axis_size("weight")
    return lax.ppermute(values, "weight", [(i, i ^ distance) for i in range(count)])


def shift_weight(values, distance):
    count = lax.axis_size("weight")
    return lax.ppermute(values, "weight", [(i, (i + distance) % count) for i in range(count)])


def gather_expert(block):
    count = lax.axis_size("expert")
    if count != 8:
        return [block] + [swap(block, r) for r in range(1, count)]
    half = block.shape[0] // 2
    from_x = swap(block, 2)
    from_y = swap(block, 4)
    diagonal = jnp.concatenate([swap(from_y[:half], 2), swap(from_x[half:], 4)], axis=0)
    return [
        block,
        swap(block, 1),
        from_x,
        swap(from_x, 1),
        from_y,
        swap(from_y, 1),
        diagonal,
        swap(diagonal, 1),
    ]


def scatter_expert(parts):
    count = lax.axis_size("expert")
    if count != 8:
        total = parts[0].astype(F32)
        for r in range(1, count):
            total = total + swap(parts[r], r).astype(F32)
        return total
    sums = {r: parts[r].astype(F32) + swap(parts[r ^ 1], 1).astype(F32) for r in (6, 2, 4, 0)}
    half = sums[6].shape[0] // 2
    far = sums[6].astype(BF)
    over_x = swap(far[:half], 2).astype(F32)
    over_y = swap(far[half:], 4).astype(F32)
    to_y = jnp.concatenate([sums[4][:half] + over_x, sums[4][half:]], axis=0).astype(BF)
    to_x = jnp.concatenate([sums[2][:half], sums[2][half:] + over_y], axis=0).astype(BF)
    return sums[0] + swap(to_x, 2).astype(F32) + swap(to_y, 4).astype(F32)


def sum_weight_small(values):
    distance = 1
    while distance < lax.axis_size("weight"):
        values = values + swap_weight(values, distance)
        distance = distance * 2
    return values


def scatter_weight(pick):
    count = lax.axis_size("weight")
    place = lax.axis_index("weight")
    total = pick(place).astype(F32)
    for step in range(1, count):
        total = total + shift_weight(pick((place + step) % count).astype(BF), step).astype(F32)
    return total


def gather_weight(block):
    count = lax.axis_size("weight")
    place = lax.axis_index("weight")
    rows = block.shape[0]
    whole = jnp.zeros((count * rows,) + block.shape[1:], block.dtype)
    whole = lax.dynamic_update_slice_in_dim(whole, block, place * rows, 0)
    for step in range(1, count):
        whole = lax.dynamic_update_slice_in_dim(
            whole, shift_weight(block, step), ((place - step) % count) * rows, 0
        )
    return whole


def two_parts(values):
    high = values.astype(BF)
    low = (values - high.astype(F32)).astype(BF)
    return high, low


def per_device(
    block_input,
    out_grad,
    norm_one,
    query_weight,
    key_weight,
    value_weight,
    query_gain,
    key_gain,
    output_weight,
    norm_two,
    router_weight,
    gate_weight,
    up_weight,
    down_weight,
    segment_ids,
    expert_routes,
    expert_slots,
):
    length = block_input.shape[0]
    local_width = query_weight.shape[1]
    head_count = local_width // HD
    score_scale = HD ** (-0.5)
    groups = lax.axis_size("weight")
    place = lax.axis_index("weight")
    owners = lax.axis_size("expert")
    owner = lax.axis_index("expert")
    local_experts = gate_weight.shape[0]
    first_expert = owner * local_experts
    quarter = length // groups
    col_width = D // groups

    experts = jnp.arange(EXPERTS)
    chosen = expert_routes[:, :, None] == experts[None, None, :]
    slot_table = jnp.min(jnp.where(chosen, expert_slots[:, :, None], CAP), axis=1)
    slot_wide = jnp.concatenate(
        [slot_table.astype(BF), jnp.full((length, EXTRA - EXPERTS), CAP, BF)], axis=1
    )
    cotangent = jnp.concatenate([out_grad.astype(BF), slot_wide], axis=1)
    cotangents = gather_expert(cotangent)

    inputs = block_input.astype(F32)
    scale_one = rms_scale(inputs)
    normed_one = (inputs * scale_one * norm_one).astype(BF)
    query_pre = dot32(normed_one, query_weight)
    key_pre = dot32(normed_one, key_weight)
    squares = jnp.stack(
        [jnp.sum(query_pre * query_pre, axis=-1), jnp.sum(key_pre * key_pre, axis=-1)]
    )
    squares = sum_weight_small(squares)
    value_flat = dot32(normed_one, value_weight).astype(BF)
    query_scale = lax.rsqrt(squares[0] / D + norm_eps)[:, None]
    key_scale = lax.rsqrt(squares[1] / D + norm_eps)[:, None]
    query_gains = query_gain.reshape(-1)
    key_gains = key_gain.reshape(-1)
    head_shape = (length, head_count, HD)
    cosine, sine_table = rope_tables(length, HD)
    query_rot = rotate(
        (query_pre * query_scale * query_gains).reshape(head_shape), cosine, sine_table
    ).astype(BF)
    key_rot = rotate(
        (key_pre * key_scale * key_gains).reshape(head_shape), cosine, sine_table
    ).astype(BF)
    value_heads = value_flat.reshape(head_shape)
    segment_row = segment_ids[0]
    positions = jnp.arange(length)
    allowed = (positions[:, None] >= positions[None, :]) & (
        segment_row[:, None] == segment_row[None, :]
    )
    scores = jnp.einsum("qhd,khd->hqk", query_rot, key_rot, preferred_element_type=F32)
    scores = jnp.where(allowed[None], scores * score_scale, -1e30)
    highest = jnp.max(scores, axis=-1, keepdims=True)
    exponent = jnp.exp(scores - highest)
    denominator = jnp.sum(exponent, axis=-1, keepdims=True)
    soft = exponent / denominator
    soft_b = soft.astype(BF)
    attended = jnp.einsum("hqk,khd->qhd", soft_b, value_heads, preferred_element_type=F32)
    attended = attended.reshape(length, local_width).astype(BF)
    attention_part = dot32(attended, output_weight)

    first_row = place * quarter
    input_rows = lax.dynamic_slice_in_dim(inputs, first_row, quarter, 0)
    second = input_rows + scatter_weight(
        lambda i: lax.dynamic_slice_in_dim(attention_part, i * quarter, quarter, 0)
    )
    scale_two = rms_scale(second)
    normed_rows = (second * scale_two * norm_two).astype(BF)
    gate_rows = jax.nn.softmax(dot32(normed_rows, router_weight), axis=-1)
    token_rows = jnp.concatenate([normed_rows, *two_parts(gate_rows)], axis=1)
    tokens_own = gather_weight(token_rows)
    tokens = gather_expert(tokens_own)

    stacked_tokens = jnp.stack(tokens)
    stacked_cotangents = jnp.stack(cotangents)
    slots = lax.dynamic_slice_in_dim(
        stacked_cotangents[:, :, D : D + EXPERTS], first_expert, local_experts, 2
    )
    picks = (slots[..., None] == jnp.arange(CAP).astype(BF)).astype(BF)
    rows_in = jnp.einsum("stec,std->secd", picks, stacked_tokens, preferred_element_type=F32).astype(BF)
    rows_grad = jnp.einsum(
        "stec,std->secd", picks, stacked_cotangents[:, :, :D], preferred_element_type=F32
    ).astype(BF)
    own_column = (experts[None, :] == (first_expert + jnp.arange(local_experts))[:, None]).astype(F32)
    row_gates = jnp.einsum("secx,ex->sec", rows_in[..., D : D + EXPERTS].astype(F32), own_column) + jnp.einsum(
        "secx,ex->sec", rows_in[..., D + EXPERTS :].astype(F32), own_column
    )
    row_gates = row_gates[..., None]
    rows_in = rows_in[..., :D]
    gate_pre = jnp.einsum("secd,edf->secf", rows_in, gate_weight, preferred_element_type=F32)
    up_pre = jnp.einsum("secd,edf->secf", rows_in, up_weight, preferred_element_type=F32)
    grad_hidden = jnp.einsum("secd,efd->secf", rows_grad, down_weight, preferred_element_type=F32)
    sigmoid_gate = jax.nn.sigmoid(gate_pre)
    silu_gate = gate_pre * sigmoid_gate
    hidden = silu_gate * up_pre
    gated_hidden = (row_gates * hidden).astype(BF)
    row_gate_grads = jnp.sum(hidden * grad_hidden, axis=-1)
    grad_hidden = row_gates * grad_hidden
    grad_gate_pre = (
        grad_hidden * up_pre * sigmoid_gate * (1.0 + gate_pre * (1.0 - sigmoid_gate))
    ).astype(BF)
    grad_up_pre = (grad_hidden * silu_gate).astype(BF)
    rows_out = jnp.einsum("secf,efd->secd", gated_hidden, down_weight, preferred_element_type=F32).astype(BF)
    rows_back = (
        jnp.einsum("secf,edf->secd", grad_gate_pre, gate_weight, preferred_element_type=F32)
        + jnp.einsum("secf,edf->secd", grad_up_pre, up_weight, preferred_element_type=F32)
    ).astype(BF)
    spread = row_gate_grads[..., None] * own_column[None, :, None, :]
    rows_back = jnp.concatenate([rows_back, *two_parts(spread)], axis=-1)
    back = jnp.einsum("stec,secd->std", picks, rows_back, preferred_element_type=F32).astype(BF)
    mixed_out = jnp.einsum("stec,secd->std", picks, rows_out, preferred_element_type=F32).astype(BF)
    down_result = jnp.einsum("secf,secd->efd", gated_hidden, rows_grad, preferred_element_type=F32)
    gate_result = jnp.einsum("secd,secf->edf", rows_in, grad_gate_pre, preferred_element_type=F32)
    up_result = jnp.einsum("secd,secf->edf", rows_in, grad_up_pre, preferred_element_type=F32)

    back_own = scatter_expert([back[r] for r in range(owners)])
    mixture_own = scatter_expert([mixed_out[r] for r in range(owners)])
    back_rows = scatter_weight(
        lambda i: lax.dynamic_slice_in_dim(back_own, i * quarter, quarter, 0)
    )
    mixture_own = lax.dynamic_update_slice_in_dim(
        mixture_own, lax.dynamic_slice_in_dim(mixture_own, first_row, quarter, 0) + second, first_row, 0
    )
    block_output = scatter_weight(
        lambda i: lax.dynamic_slice_in_dim(mixture_own, i * col_width, col_width, 1)
    )

    grad_probs = back_rows[:, D : D + EXPERTS] + back_rows[:, D + EXPERTS :]
    grad_logits = gate_rows * (grad_probs - jnp.sum(gate_rows * grad_probs, axis=-1, keepdims=True))
    grad_logits_b = grad_logits.astype(BF)
    grad_normed_two = back_rows[:, :D] + dot32(grad_logits_b, router_weight.T)
    weighted_two = grad_normed_two * norm_two
    norm_two_part = sum_weight_small(jnp.sum(grad_normed_two * second * scale_two, axis=0))
    out_grad_rows = lax.dynamic_slice_in_dim(out_grad, first_row, quarter, 0)
    grad_second = (
        out_grad_rows
        + scale_two * weighted_two
        - second * scale_two**3 * jnp.mean(second * weighted_two, axis=-1, keepdims=True)
    )
    second_rows = jnp.concatenate(
        [grad_second.astype(BF), grad_logits_b, jnp.zeros((quarter, EXTRA - EXPERTS), BF)], axis=1
    )
    second_all = gather_weight(second_rows)
    grad_second_b = second_all[:, :D]

    router_cols = EXPERTS // groups
    logits_mine = lax.dynamic_slice_in_dim(second_all, D + place * router_cols, router_cols, 1)
    router_part = dot32(tokens_own[:, :D].T, logits_mine)
    output_part = dot32(grad_second_b.T, attended)
    grad_mixed = dot32(grad_second_b, output_weight.T).astype(BF).reshape(head_shape)
    grad_soft = jnp.einsum("qhd,khd->hqk", grad_mixed, value_heads, preferred_element_type=F32)
    inner = jnp.sum(soft * grad_soft, axis=-1, keepdims=True)
    grad_scores = (soft * (grad_soft - inner)).astype(BF)
    grad_query_rot = (
        jnp.einsum("hqk,khd->qhd", grad_scores, key_rot, preferred_element_type=F32) * score_scale
    )
    grad_key_rot = (
        jnp.einsum("hqk,qhd->khd", grad_scores, query_rot, preferred_element_type=F32) * score_scale
    )
    grad_values = jnp.einsum("hqk,qhd->khd", soft_b, grad_mixed, preferred_element_type=F32)
    grad_values_b = grad_values.reshape(length, local_width).astype(BF)
    grad_query_norm = rotate_back(grad_query_rot, cosine, sine_table).reshape(length, local_width)
    grad_key_norm = rotate_back(grad_key_rot, cosine, sine_table).reshape(length, local_width)
    weighted_query = grad_query_norm * query_gains
    weighted_key = grad_key_norm * key_gains
    query_gain_part = jnp.sum(grad_query_norm * query_pre * query_scale, axis=0)
    key_gain_part = jnp.sum(grad_key_norm * key_pre * key_scale, axis=0)
    cross = jnp.stack(
        [jnp.sum(query_pre * weighted_query, axis=-1), jnp.sum(key_pre * weighted_key, axis=-1)]
    )
    cross = sum_weight_small(cross)
    grad_query_pre = (
        query_scale * weighted_query - query_pre * query_scale**3 * (cross[0] / D)[:, None]
    ).astype(BF)
    grad_key_pre = (
        key_scale * weighted_key - key_pre * key_scale**3 * (cross[1] / D)[:, None]
    ).astype(BF)
    query_part = dot32(normed_one.T, grad_query_pre)
    key_part = dot32(normed_one.T, grad_key_pre)
    value_part = dot32(normed_one.T, grad_values_b)
    grad_normed_local = (
        dot32(grad_query_pre, query_weight.T)
        + dot32(grad_key_pre, key_weight.T)
        + dot32(grad_values_b, value_weight.T)
    )
    norm_one_part = sum_weight_small(jnp.sum(grad_normed_local * inputs * scale_one, axis=0))
    grad_normed_one = scatter_weight(
        lambda i: lax.dynamic_slice_in_dim(grad_normed_local, i * quarter, quarter, 0)
    )
    scale_rows = lax.dynamic_slice_in_dim(scale_one, first_row, quarter, 0)
    weighted_one = grad_normed_one * norm_one
    input_result = (
        grad_second
        + scale_rows * weighted_one
        - input_rows * scale_rows**3 * jnp.mean(input_rows * weighted_one, axis=-1, keepdims=True)
    )

    gain_width = HD // owners
    gains = jnp.concatenate(
        [query_gain_part.reshape(head_count, HD), key_gain_part.reshape(head_count, HD)], axis=0
    ).T.reshape(owners, gain_width, 2 * head_count)
    gains = jnp.pad(gains, ((0, 0), (0, D // owners - gain_width), (0, 0)))
    small = jnp.concatenate(
        [
            router_part.reshape(owners, D // owners, router_cols),
            norm_one_part.reshape(owners, D // owners, 1),
            norm_two_part.reshape(owners, D // owners, 1),
            gains,
        ],
        axis=2,
    )
    small = jnp.pad(small, ((0, 0), (0, 0), (0, EXTRA - small.shape[2])))
    combined = jnp.concatenate(
        [query_part, key_part, value_part, output_part, small.reshape(D, EXTRA)], axis=1
    ).astype(BF)
    combined = combined.reshape(owners, D // owners, combined.shape[1])
    reduced = scatter_expert(
        [lax.dynamic_index_in_dim(combined, owner ^ r, 0, keepdims=False) for r in range(owners)]
    )
    width = local_width
    tail = reduced[:, 4 * width :]
    gain_result = tail[:gain_width, router_cols + 2 : router_cols + 2 + 2 * head_count].T
    return (
        block_output,
        input_result,
        tail[:, router_cols],
        reduced[:, :width],
        reduced[:, width : 2 * width],
        reduced[:, 2 * width : 3 * width],
        gain_result[:head_count],
        gain_result[head_count:],
        reduced[:, 3 * width : 4 * width].T,
        tail[:, router_cols + 1],
        tail[:, :router_cols],
        gate_result,
        up_result,
        down_result,
    )


def solution(mesh):
    in_specs = (
        P("expert", None),
        P("expert", None),
        P(),
        P(None, "weight"),
        P(None, "weight"),
        P(None, "weight"),
        P("weight", None),
        P("weight", None),
        P("weight", None),
        P(),
        P(),
        P("expert", None, "weight"),
        P("expert", None, "weight"),
        P("expert", "weight", None),
        P("expert", None),
        P("expert", None),
        P("expert", None),
    )
    out_specs = (
        P("expert", "weight"),
        P(("expert", "weight"), None),
        P("expert"),
        P("expert", "weight"),
        P("expert", "weight"),
        P("expert", "weight"),
        P("weight", "expert"),
        P("weight", "expert"),
        P("weight", "expert"),
        P("expert"),
        P("expert", "weight"),
        P("expert", None, "weight"),
        P("expert", None, "weight"),
        P("expert", "weight", None),
    )
    return jax.shard_map(
        per_device, mesh=mesh, in_specs=in_specs, out_specs=out_specs, check_vma=False
    )
```

```python
import functools

import jax
import jax.numpy as jnp
from jax import lax
from jax.experimental import pallas as pl
from jax.experimental.pallas import tpu as pltpu
from jax.sharding import PartitionSpec as P

D = 2048
HD = 128
EXPERTS = 64
CAP = 96
EXTRA = 128
WIDE = D + EXTRA
BF = jnp.bfloat16
F32 = jnp.float32
NT = (((1,), (1,)), ((), ()))
VMEM_BYTES = 67_000_000

norm_eps = 1e-05
rope_base = 10000.0


def rms_scale(values):
    return lax.rsqrt(jnp.mean(values * values, axis=-1, keepdims=True) + norm_eps)


def rope_tables(length, head_width):
    exponent = jnp.arange(head_width // 2).astype(F32) * 2.0 / head_width
    inverse = rope_base ** (-exponent)
    angles = jnp.arange(length).astype(F32)[:, None] * inverse[None, :]
    angles = jnp.concatenate([angles, angles], axis=-1)[:, None, :]
    return (jnp.cos(angles), jnp.sin(angles))


def rotate(values, cosine, sine_table):
    half_width = values.shape[-1] // 2
    turned = jnp.concatenate([-values[..., half_width:], values[..., :half_width]], axis=-1)
    return values * cosine + turned * sine_table


def rotate_back(values, cosine, sine_table):
    half_width = values.shape[-1] // 2
    shifted = values * sine_table
    turned = jnp.concatenate([shifted[..., half_width:], -shifted[..., :half_width]], axis=-1)
    return values * cosine + turned


def dot32(left, right):
    return jnp.dot(left, right, preferred_element_type=F32)


def swap(values, distance):
    count = lax.axis_size("expert")
    return lax.ppermute(values, "expert", [(i, i ^ distance) for i in range(count)])


def swap_weight(values, distance):
    count = lax.axis_size("weight")
    return lax.ppermute(values, "weight", [(i, i ^ distance) for i in range(count)])


def shift_weight(values, distance):
    count = lax.axis_size("weight")
    return lax.ppermute(values, "weight", [(i, (i + distance) % count) for i in range(count)])


def gather_start(block):
    if lax.axis_size("expert") != 8:
        return ()
    return (swap(block, 2), swap(block, 4))


def gather_finish(block, near):
    count = lax.axis_size("expert")
    if count != 8:
        return [block] + [swap(block, r) for r in range(1, count)]
    half = block.shape[0] // 2
    from_x, from_y = near
    diagonal = jnp.concatenate([swap(from_y[:half], 2), swap(from_x[half:], 4)], axis=0)
    return [
        block,
        swap(block, 1),
        from_x,
        swap(from_x, 1),
        from_y,
        swap(from_y, 1),
        diagonal,
        swap(diagonal, 1),
    ]


def scatter_expert(parts):
    count = lax.axis_size("expert")
    if count != 8:
        total = parts[0].astype(F32)
        for r in range(1, count):
            total = total + swap(parts[r], r).astype(F32)
        return total
    sums = {r: parts[r].astype(F32) + swap(parts[r ^ 1], 1).astype(F32) for r in (6, 2, 4, 0)}
    half = sums[6].shape[0] // 2
    far = sums[6].astype(BF)
    over_x = swap(far[:half], 2).astype(F32)
    over_y = swap(far[half:], 4).astype(F32)
    to_y = jnp.concatenate([sums[4][:half] + over_x, sums[4][half:]], axis=0).astype(BF)
    to_x = jnp.concatenate([sums[2][:half], sums[2][half:] + over_y], axis=0).astype(BF)
    return sums[0] + swap(to_x, 2).astype(F32) + swap(to_y, 4).astype(F32)


def sum_weight_small(values):
    distance = 1
    while distance < lax.axis_size("weight"):
        values = values + swap_weight(values, distance)
        distance = distance * 2
    return values


def scatter_weight(pick):
    count = lax.axis_size("weight")
    place = lax.axis_index("weight")
    total = pick(place).astype(F32)
    for step in range(1, count):
        total = total + shift_weight(pick((place + step) % count).astype(BF), step).astype(F32)
    return total


def gather_weight(block):
    count = lax.axis_size("weight")
    place = lax.axis_index("weight")
    rows = block.shape[0]
    whole = jnp.zeros((count * rows,) + block.shape[1:], block.dtype)
    whole = lax.dynamic_update_slice_in_dim(whole, block, place * rows, 0)
    for step in range(1, count):
        whole = lax.dynamic_update_slice_in_dim(
            whole, shift_weight(block, step), ((place - step) % count) * rows, 0
        )
    return whole


def two_parts(values):
    high = values.astype(BF)
    low = (values - high.astype(F32)).astype(BF)
    return high, low


def dot_nt(left, right):
    return lax.dot_general(left, right, NT, preferred_element_type=F32)


def row_places(shape, axis, first_expert):
    row = lax.broadcasted_iota(jnp.int32, shape, axis)
    expert = (row * 683) >> 16
    return first_expert + expert, row - expert * CAP


def pick_matrix(table, local_experts, first_expert):
    rows = local_experts * CAP
    expert, _ = row_places((rows, EXTRA), 0, first_expert)
    lane = lax.broadcasted_iota(jnp.int32, (rows, EXTRA), 1)
    wanted = dot_nt((lane == expert).astype(BF), table)
    _, slot = row_places(wanted.shape, 0, first_expert)
    return (wanted == slot.astype(F32)).astype(BF)


def put_matrix(table, local_experts, first_expert):
    rows = local_experts * CAP
    expert, _ = row_places((EXTRA, rows), 1, first_expert)
    lane = lax.broadcasted_iota(jnp.int32, (EXTRA, rows), 0)
    wanted = dot32(table, (lane == expert).astype(BF))
    _, slot = row_places(wanted.shape, 1, first_expert)
    return (wanted == slot.astype(F32)).astype(BF)


def prepare_kernel(grad_ref, slot_ref, out_ref):
    out_ref[:, :D] = grad_ref[...].astype(BF)
    out_ref[:, D:] = slot_ref[...]


def prepare_call(out_grad, slot_wide):
    length = out_grad.shape[0]
    rows = length // 4
    return pl.pallas_call(
        prepare_kernel,
        grid=(4,),
        in_specs=[pl.BlockSpec((rows, D), lambda i: (i, 0)), pl.BlockSpec((rows, EXTRA), lambda i: (i, 0))],
        out_specs=pl.BlockSpec((rows, WIDE), lambda i: (i, 0)),
        out_shape=jax.ShapeDtypeStruct((length, WIDE), BF),
        cost_estimate=pl.CostEstimate(
            flops=length * D, transcendentals=0, bytes_accessed=length * WIDE * 6
        ),
        name="prepare_cotangent",
    )(out_grad, slot_wide)


def cotangent_kernel(seqs, local_experts, first_ref, *refs):
    cots = refs[:seqs]
    down_ref = refs[seqs]
    rows_ref, hidden_ref, held = refs[seqs + 1 :]
    e = pl.program_id(0)
    first = first_ref[0]

    @pl.when(e == 0)
    def _():
        for s in range(seqs):
            pick = pick_matrix(cots[s][:, D:], local_experts, first)
            held[s] = dot32(pick, cots[s][:, :D]).astype(BF)

    rows = held[:, pl.ds(pl.multiple_of(e * CAP, CAP), CAP), :]
    rows_ref[:, 0] = rows
    hidden_ref[:, 0] = dot_nt(rows.reshape(seqs * CAP, D), down_ref[0]).reshape(seqs, CAP, -1)


def cotangent_call(first, cots, down_weight):
    seqs = len(cots)
    local_experts, width, _ = down_weight.shape
    length = cots[0].shape[0]
    whole = pl.BlockSpec((length, WIDE), lambda e, f: (0, 0), pipeline_mode=pl.Buffered(1))
    return pl.pallas_call(
        functools.partial(cotangent_kernel, seqs, local_experts),
        grid_spec=pltpu.PrefetchScalarGridSpec(
            num_scalar_prefetch=1,
            grid=(local_experts,),
            in_specs=[whole] * seqs + [pl.BlockSpec((1, width, D), lambda e, f: (e, 0, 0))],
            out_specs=[
                pl.BlockSpec((seqs, 1, CAP, D), lambda e, f: (0, e, 0, 0)),
                pl.BlockSpec((seqs, 1, CAP, width), lambda e, f: (0, e, 0, 0)),
            ],
            scratch_shapes=[pltpu.VMEM((seqs, local_experts * CAP, D), BF)],
        ),
        out_shape=[
            jax.ShapeDtypeStruct((seqs, local_experts, CAP, D), BF),
            jax.ShapeDtypeStruct((seqs, local_experts, CAP, width), F32),
        ],
        compiler_params=pltpu.CompilerParams(
            dimension_semantics=("arbitrary",), vmem_limit_bytes=VMEM_BYTES
        ),
        cost_estimate=pl.CostEstimate(
            flops=2 * seqs * local_experts * CAP * D * (length + width),
            transcendentals=0,
            bytes_accessed=seqs * (length * WIDE + local_experts * CAP * (D + 2 * width)) * 2
            + local_experts * width * D * 2,
        ),
        name="cotangent_rows",
    )(first, *cots, down_weight)


def expert_kernel(seqs, local_experts, extra, first_ref, *refs):
    tokens = refs[:seqs]
    tables = refs[seqs : 2 * seqs]
    grad_ref, gate_ref, up_ref, down_ref = refs[2 * seqs : 2 * seqs + 4]
    rest = refs[2 * seqs + 4 + extra :]
    rows_ref, hidden_ref, grad_gate_ref, grad_up_ref = rest[:4]
    backs = rest[4 : 4 + seqs]
    mixes = rest[4 + seqs : 4 + 2 * seqs]
    held, out_rows = rest[4 + 2 * seqs :]
    e = pl.program_id(0)
    first = first_ref[0]
    count = seqs * CAP

    @pl.when(e == 0)
    def _():
        for s in range(seqs):
            pick = pick_matrix(tables[s][...], local_experts, first)
            held[s] = dot32(pick, tokens[s][...]).astype(BF)

    span = pl.ds(pl.multiple_of(e * CAP, CAP), CAP)
    both = held[:, span, :].reshape(count, WIDE)
    rows = both[:, :D]
    rows_ref[:, 0] = rows.reshape(seqs, CAP, D)
    lane = lax.broadcasted_iota(jnp.int32, (count, EXTRA), 1)
    own_high = lane == first + e
    own_low = lane == first + e + EXPERTS
    gates = jnp.sum(
        jnp.where(own_high | own_low, both[:, D:].astype(F32), 0.0), axis=1, keepdims=True
    )
    gate_pre = dot32(rows, gate_ref[0])
    up_pre = dot32(rows, up_ref[0])
    grad_hidden = grad_ref[:, 0].reshape(count, -1)
    sigmoid_gate = jax.nn.sigmoid(gate_pre)
    silu_gate = gate_pre * sigmoid_gate
    hidden = silu_gate * up_pre
    gated = (gates * hidden).astype(BF)
    gate_grads = jnp.sum(hidden * grad_hidden, axis=1, keepdims=True)
    grad_hidden = gates * grad_hidden
    grad_gate = (
        grad_hidden * up_pre * sigmoid_gate * (1.0 + gate_pre * (1.0 - sigmoid_gate))
    ).astype(BF)
    grad_up = (grad_hidden * silu_gate).astype(BF)
    hidden_ref[:, 0] = gated.reshape(seqs, CAP, -1)
    grad_gate_ref[:, 0] = grad_gate.reshape(seqs, CAP, -1)
    grad_up_ref[:, 0] = grad_up.reshape(seqs, CAP, -1)
    out_rows[:, span, :] = dot32(gated, down_ref[0]).astype(BF).reshape(seqs, CAP, D)
    back = dot_nt(grad_gate, gate_ref[0]) + dot_nt(grad_up, up_ref[0])
    held[:, span, :D] = back.astype(BF).reshape(seqs, CAP, D)
    high = gate_grads.astype(BF).astype(F32)
    spread = jnp.where(own_high, high, jnp.where(own_low, gate_grads - high, 0.0))
    held[:, span, D:] = spread.astype(BF).reshape(seqs, CAP, EXTRA)

    @pl.when(e == local_experts - 1)
    def _():
        for s in range(seqs):
            put = put_matrix(tables[s][...], local_experts, first)
            backs[s][...] = dot32(put, held[s]).astype(BF)
            mixes[s][...] = dot32(put, out_rows[s]).astype(BF)


def expert_call(first, tokens, cots, grads, gate_weight, up_weight, down_weight, after):
    seqs = len(tokens)
    local_experts, width, _ = down_weight.shape
    length = tokens[0].shape[0]
    rows = local_experts * CAP
    once = pl.Buffered(1)
    per_expert = lambda last: pl.BlockSpec((seqs, 1, CAP, last), lambda e, f: (0, e, 0, 0))
    return pl.pallas_call(
        functools.partial(expert_kernel, seqs, local_experts, len(after)),
        grid_spec=pltpu.PrefetchScalarGridSpec(
            num_scalar_prefetch=1,
            grid=(local_experts,),
            in_specs=[pl.BlockSpec((length, WIDE), lambda e, f: (0, 0), pipeline_mode=once)] * seqs
            + [pl.BlockSpec((length, EXTRA), lambda e, f: (0, D // EXTRA), pipeline_mode=once)] * seqs
            + [
                per_expert(width),
                pl.BlockSpec((1, D, width), lambda e, f: (e, 0, 0)),
                pl.BlockSpec((1, D, width), lambda e, f: (e, 0, 0)),
                pl.BlockSpec((1, width, D), lambda e, f: (e, 0, 0)),
            ]
            + [pl.BlockSpec(memory_space=pl.ANY)] * len(after),
            out_specs=[per_expert(D), per_expert(width), per_expert(width), per_expert(width)]
            + [pl.BlockSpec((length, WIDE), lambda e, f: (0, 0), pipeline_mode=once)] * seqs
            + [pl.BlockSpec((length, D), lambda e, f: (0, 0), pipeline_mode=once)] * seqs,
            scratch_shapes=[pltpu.VMEM((seqs, rows, WIDE), BF), pltpu.VMEM((seqs, rows, D), BF)],
        ),
        out_shape=[jax.ShapeDtypeStruct((seqs, local_experts, CAP, D), BF)]
        + [jax.ShapeDtypeStruct((seqs, local_experts, CAP, width), BF)] * 3
        + [jax.ShapeDtypeStruct((length, WIDE), BF)] * seqs
        + [jax.ShapeDtypeStruct((length, D), BF)] * seqs,
        compiler_params=pltpu.CompilerParams(
            dimension_semantics=("arbitrary",), vmem_limit_bytes=VMEM_BYTES
        ),
        cost_estimate=pl.CostEstimate(
            flops=2 * seqs * rows * D * (3 * length + 5 * width),
            transcendentals=seqs * rows * width,
            bytes_accessed=seqs * (3 * length * WIDE + rows * (D + 5 * width)) * 2
            + 3 * local_experts * width * D * 2,
        ),
        name="expert_rows",
    )(first, *tokens, *cots, grads, gate_weight, up_weight, down_weight, *after)


def weight_grad_kernel(parts, *refs):
    ins, (gate_ref, up_ref, down_ref), (rows, cots, small) = (
        refs[: 5 * parts],
        refs[5 * parts : 5 * parts + 3],
        refs[5 * parts + 3 :],
    )
    width = gate_ref.shape[2]
    for p in range(parts):
        rows_ref, cot_ref, hidden_ref, grad_gate_ref, grad_up_ref = ins[5 * p : 5 * p + 5]
        count = rows_ref.shape[0] * CAP
        span = pl.ds(p * count, count)
        rows[span] = rows_ref[:, 0].reshape(count, D)
        cots[span] = cot_ref[:, 0].reshape(count, D)
        small[span, :width] = grad_gate_ref[:, 0].reshape(count, width)
        small[span, width : 2 * width] = grad_up_ref[:, 0].reshape(count, width)
        small[span, 2 * width :] = hidden_ref[:, 0].reshape(count, width)
    both = dot32(rows[...].T, small[:, : 2 * width])
    gate_ref[0] = both[:, :width]
    up_ref[0] = both[:, width:]
    down_ref[0] = dot32(small[:, 2 * width :].T, cots[...])


def weight_grads(pieces):
    seqs, local_experts, _, width = pieces[0][2].shape
    if lax.axis_size("expert") != 8:
        rows, cots, hidden, grad_gate, grad_up = (
            jnp.concatenate([piece[i] for piece in pieces], axis=0) for i in range(5)
        )
        return (
            jnp.einsum("secd,secf->edf", rows, grad_gate, preferred_element_type=F32),
            jnp.einsum("secd,secf->edf", rows, grad_up, preferred_element_type=F32),
            jnp.einsum("secf,secd->efd", hidden, cots, preferred_element_type=F32),
        )
    total = len(pieces) * seqs * CAP
    block = lambda last: pl.BlockSpec((seqs, 1, CAP, last), lambda e: (0, e, 0, 0))
    flat = [array for piece in pieces for array in piece]
    return pl.pallas_call(
        functools.partial(weight_grad_kernel, len(pieces)),
        grid=(local_experts,),
        in_specs=[block(D), block(D), block(width), block(width), block(width)] * len(pieces),
        out_specs=[
            pl.BlockSpec((1, D, width), lambda e: (e, 0, 0)),
            pl.BlockSpec((1, D, width), lambda e: (e, 0, 0)),
            pl.BlockSpec((1, width, D), lambda e: (e, 0, 0)),
        ],
        out_shape=[
            jax.ShapeDtypeStruct((local_experts, D, width), F32),
            jax.ShapeDtypeStruct((local_experts, D, width), F32),
            jax.ShapeDtypeStruct((local_experts, width, D), F32),
        ],
        scratch_shapes=[
            pltpu.VMEM((total, D), BF),
            pltpu.VMEM((total, D), BF),
            pltpu.VMEM((total, 3 * width), BF),
        ],
        compiler_params=pltpu.CompilerParams(
            dimension_semantics=("arbitrary",), vmem_limit_bytes=VMEM_BYTES
        ),
        cost_estimate=pl.CostEstimate(
            flops=6 * local_experts * total * D * width,
            transcendentals=0,
            bytes_accessed=local_experts * (total * (2 * D + 3 * width) * 2 + 3 * D * width * 4),
        ),
        name="weight_grads",
    )(*flat)


def layer(
    block_input,
    out_grad,
    norm_one,
    query_weight,
    key_weight,
    value_weight,
    query_gain,
    key_gain,
    output_weight,
    norm_two,
    router_weight,
    gate_weight,
    up_weight,
    down_weight,
    segment_ids,
    expert_routes,
    expert_slots,
):
    length = block_input.shape[0]
    local_width = query_weight.shape[1]
    head_count = local_width // HD
    score_scale = HD ** (-0.5)
    groups = lax.axis_size("weight")
    place = lax.axis_index("weight")
    owners = lax.axis_size("expert")
    owner = lax.axis_index("expert")
    local_experts = gate_weight.shape[0]
    first_expert = owner * local_experts
    quarter = length // groups
    col_width = D // groups

    chosen = expert_routes[:, :, None] == jnp.arange(EXPERTS)[None, None, :]
    slot_table = jnp.min(jnp.where(chosen, expert_slots[:, :, None], CAP), axis=1)
    slot_wide = jnp.concatenate(
        [slot_table.astype(BF), jnp.full((length, EXTRA - EXPERTS), CAP, BF)], axis=1
    )

    inputs = block_input.astype(F32)
    scale_one = rms_scale(inputs)
    normed_one = (inputs * scale_one * norm_one).astype(BF)
    query_pre = dot32(normed_one, query_weight)
    key_pre = dot32(normed_one, key_weight)
    squares = jnp.stack(
        [jnp.sum(query_pre * query_pre, axis=-1), jnp.sum(key_pre * key_pre, axis=-1)]
    )
    squares = sum_weight_small(squares)
    cotangent = prepare_call(out_grad, slot_wide)
    cotangents_near = gather_start(cotangent)
    value_flat = dot32(normed_one, value_weight).astype(BF)
    query_scale = lax.rsqrt(squares[0] / D + norm_eps)[:, None]
    key_scale = lax.rsqrt(squares[1] / D + norm_eps)[:, None]
    query_gains = query_gain.reshape(-1)
    key_gains = key_gain.reshape(-1)
    head_shape = (length, head_count, HD)
    cosine, sine_table = rope_tables(length, HD)
    query_rot = rotate(
        (query_pre * query_scale * query_gains).reshape(head_shape), cosine, sine_table
    ).astype(BF)
    key_rot = rotate(
        (key_pre * key_scale * key_gains).reshape(head_shape), cosine, sine_table
    ).astype(BF)
    value_heads = value_flat.reshape(head_shape)
    segment_row = segment_ids[0]
    positions = jnp.arange(length)
    allowed = (positions[:, None] >= positions[None, :]) & (
        segment_row[:, None] == segment_row[None, :]
    )
    scores = jnp.einsum("qhd,khd->hqk", query_rot, key_rot, preferred_element_type=F32)
    scores = jnp.where(allowed[None], scores * score_scale, -1e30)
    highest = jnp.max(scores, axis=-1, keepdims=True)
    exponent = jnp.exp(scores - highest)
    denominator = jnp.sum(exponent, axis=-1, keepdims=True)
    soft = exponent / denominator
    soft_b = soft.astype(BF)
    attended = jnp.einsum("hqk,khd->qhd", soft_b, value_heads, preferred_element_type=F32)
    attended = attended.reshape(length, local_width).astype(BF)
    attention_part = dot32(attended, output_weight).astype(BF)
    cotangents = gather_finish(cotangent, cotangents_near)

    first_row = place * quarter
    input_rows = lax.dynamic_slice_in_dim(block_input, first_row, quarter, 0).astype(F32)
    second = input_rows + scatter_weight(
        lambda i: lax.dynamic_slice_in_dim(attention_part, i * quarter, quarter, 0)
    )
    scale_two = rms_scale(second)
    normed_rows = (second * scale_two * norm_two).astype(BF)
    gate_rows = jax.nn.softmax(dot32(normed_rows, router_weight), axis=-1)
    token_rows = jnp.concatenate([normed_rows, *two_parts(gate_rows)], axis=1)
    tokens_own = gather_weight(token_rows)
    tokens = gather_finish(tokens_own, gather_start(tokens_own))

    first_array = jnp.full((1,), first_expert, jnp.int32)
    pairs = [(r, r + 1) for r in range(0, owners, 2)]
    if owners == 8:
        pairs = [(0, 1), (2, 3), (6, 7), (4, 5)]
    cot_rows = {}
    for pair in pairs:
        cot_rows[pair] = cotangent_call(first_array, [cotangents[r] for r in pair], down_weight)
    after = []
    back, mixed_out, pieces = {}, {}, []
    for pair in pairs:
        rows_grad, grad_hidden = cot_rows[pair]
        rows_in, hidden, grad_gate, grad_up, *both = expert_call(
            first_array,
            [tokens[r] for r in pair],
            [cotangents[r] for r in pair],
            grad_hidden,
            gate_weight,
            up_weight,
            down_weight,
            after,
        )
        after = [hidden]
        pieces.append((rows_in, rows_grad, hidden, grad_gate, grad_up))
        for i, r in enumerate(pair):
            back[r] = both[i]
            mixed_out[r] = both[len(pair) + i]
    gate_result, up_result, down_result = weight_grads(pieces)

    back_own = scatter_expert([back[r] for r in range(owners)])
    own_rows = lax.dynamic_slice_in_dim(mixed_out[0], first_row, quarter, 0).astype(F32) + second
    mixed_out[0] = lax.dynamic_update_slice_in_dim(mixed_out[0], own_rows.astype(BF), first_row, 0)
    mixed_list = [mixed_out[r] for r in range(owners)]
    mixed_list, back_own = lax.optimization_barrier((mixed_list, back_own))
    mixture_own = scatter_expert(mixed_list)
    back_rows = scatter_weight(
        lambda i: lax.dynamic_slice_in_dim(back_own, i * quarter, quarter, 0)
    )
    block_output = scatter_weight(
        lambda i: lax.dynamic_slice_in_dim(mixture_own, i * col_width, col_width, 1)
    )

    grad_probs = back_rows[:, D : D + EXPERTS] + back_rows[:, D + EXPERTS :]
    grad_logits = gate_rows * (grad_probs - jnp.sum(gate_rows * grad_probs, axis=-1, keepdims=True))
    grad_logits_b = grad_logits.astype(BF)
    grad_normed_two = back_rows[:, :D] + dot32(grad_logits_b, router_weight.T)
    weighted_two = grad_normed_two * norm_two
    norm_two_part = sum_weight_small(jnp.sum(grad_normed_two * second * scale_two, axis=0))
    out_grad_rows = lax.dynamic_slice_in_dim(out_grad, first_row, quarter, 0)
    grad_second = (
        out_grad_rows
        + scale_two * weighted_two
        - second * scale_two**3 * jnp.mean(second * weighted_two, axis=-1, keepdims=True)
    )
    second_rows = jnp.concatenate(
        [grad_second.astype(BF), grad_logits_b, jnp.zeros((quarter, EXTRA - EXPERTS), BF)], axis=1
    )
    second_all = gather_weight(second_rows)
    grad_second_b = second_all[:, :D]

    router_cols = EXPERTS // groups
    logits_mine = lax.dynamic_slice_in_dim(second_all, D + place * router_cols, router_cols, 1)
    router_part = dot32(tokens_own[:, :D].T, logits_mine)
    output_part = dot32(grad_second_b.T, attended)
    grad_mixed = dot32(grad_second_b, output_weight.T).astype(BF).reshape(head_shape)
    grad_soft = jnp.einsum("qhd,khd->hqk", grad_mixed, value_heads, preferred_element_type=F32)
    inner = jnp.sum(soft * grad_soft, axis=-1, keepdims=True)
    grad_scores = (soft * (grad_soft - inner)).astype(BF)
    grad_query_rot = (
        jnp.einsum("hqk,khd->qhd", grad_scores, key_rot, preferred_element_type=F32) * score_scale
    )
    grad_key_rot = (
        jnp.einsum("hqk,qhd->khd", grad_scores, query_rot, preferred_element_type=F32) * score_scale
    )
    grad_values = jnp.einsum("hqk,qhd->khd", soft_b, grad_mixed, preferred_element_type=F32)
    grad_values_b = grad_values.reshape(length, local_width).astype(BF)
    grad_query_norm = rotate_back(grad_query_rot, cosine, sine_table).reshape(length, local_width)
    grad_key_norm = rotate_back(grad_key_rot, cosine, sine_table).reshape(length, local_width)
    weighted_query = grad_query_norm * query_gains
    weighted_key = grad_key_norm * key_gains
    query_gain_part = jnp.sum(grad_query_norm * query_pre * query_scale, axis=0)
    key_gain_part = jnp.sum(grad_key_norm * key_pre * key_scale, axis=0)
    cross = jnp.stack(
        [jnp.sum(query_pre * weighted_query, axis=-1), jnp.sum(key_pre * weighted_key, axis=-1)]
    )
    cross = sum_weight_small(cross)
    grad_query_pre = (
        query_scale * weighted_query - query_pre * query_scale**3 * (cross[0] / D)[:, None]
    ).astype(BF)
    grad_key_pre = (
        key_scale * weighted_key - key_pre * key_scale**3 * (cross[1] / D)[:, None]
    ).astype(BF)
    query_part = dot32(normed_one.T, grad_query_pre)
    key_part = dot32(normed_one.T, grad_key_pre)
    value_part = dot32(normed_one.T, grad_values_b)
    grad_normed_local = (
        dot32(grad_query_pre, query_weight.T)
        + dot32(grad_key_pre, key_weight.T)
        + dot32(grad_values_b, value_weight.T)
    )
    inputs_again = lax.optimization_barrier(block_input).astype(F32)
    norm_one_part = sum_weight_small(jnp.sum(grad_normed_local * inputs_again * scale_one, axis=0))
    grad_normed_one = scatter_weight(
        lambda i: lax.dynamic_slice_in_dim(grad_normed_local, i * quarter, quarter, 0)
    )
    scale_rows = lax.dynamic_slice_in_dim(scale_one, first_row, quarter, 0)
    weighted_one = grad_normed_one * norm_one
    input_result = (
        grad_second
        + scale_rows * weighted_one
        - input_rows * scale_rows**3 * jnp.mean(input_rows * weighted_one, axis=-1, keepdims=True)
    )

    gain_width = HD // owners
    gains = jnp.concatenate(
        [query_gain_part.reshape(head_count, HD), key_gain_part.reshape(head_count, HD)], axis=0
    ).T.reshape(owners, gain_width, 2 * head_count)
    gains = jnp.pad(gains, ((0, 0), (0, D // owners - gain_width), (0, 0)))
    small = jnp.concatenate(
        [
            router_part.reshape(owners, D // owners, router_cols),
            norm_one_part.reshape(owners, D // owners, 1),
            norm_two_part.reshape(owners, D // owners, 1),
            gains,
        ],
        axis=2,
    )
    small = jnp.pad(small, ((0, 0), (0, 0), (0, EXTRA - small.shape[2])))
    combined = jnp.concatenate(
        [query_part, key_part, value_part, output_part, small.reshape(D, EXTRA)], axis=1
    ).astype(BF)
    combined = combined.reshape(owners, D // owners, combined.shape[1])
    reduced = scatter_expert(
        [lax.dynamic_index_in_dim(combined, owner ^ r, 0, keepdims=False) for r in range(owners)],
    )
    width = local_width
    tail = reduced[:, 4 * width :]
    gain_result = tail[:gain_width, router_cols + 2 : router_cols + 2 + 2 * head_count].T
    return (
        block_output,
        input_result,
        tail[:, router_cols],
        reduced[:, :width],
        reduced[:, width : 2 * width],
        reduced[:, 2 * width : 3 * width],
        gain_result[:head_count],
        gain_result[head_count:],
        reduced[:, 3 * width : 4 * width].T,
        tail[:, router_cols + 1],
        tail[:, :router_cols],
        gate_result,
        up_result,
        down_result,
    )


def solution(mesh):
    in_specs = (
        P("expert", None),
        P("expert", None),
        P(),
        P(None, "weight"),
        P(None, "weight"),
        P(None, "weight"),
        P("weight", None),
        P("weight", None),
        P("weight", None),
        P(),
        P(),
        P("expert", None, "weight"),
        P("expert", None, "weight"),
        P("expert", "weight", None),
        P("expert", None),
        P("expert", None),
        P("expert", None),
    )
    out_specs = (
        P("expert", "weight"),
        P(("expert", "weight"), None),
        P("expert"),
        P("expert", "weight"),
        P("expert", "weight"),
        P("expert", "weight"),
        P("weight", "expert"),
        P("weight", "expert"),
        P("weight", "expert"),
        P("expert"),
        P("expert", "weight"),
        P("expert", None, "weight"),
        P("expert", None, "weight"),
        P("expert", "weight", None),
    )
    return jax.shard_map(layer, mesh=mesh, in_specs=in_specs, out_specs=out_specs, check_vma=False)
```

```python
import functools

import jax
import jax.numpy as jnp
from jax import lax
from jax.experimental import pallas as pl
from jax.experimental.pallas import tpu as pltpu
from jax.sharding import PartitionSpec as P

D = 2048
HD = 128
EXPERTS = 64
CAP = 96
EXTRA = 128
WIDE = D + EXTRA
TAIL = 32
BF = jnp.bfloat16
F32 = jnp.float32
NT = (((1,), (1,)), ((), ()))
VMEM_BYTES = 67_000_000
EX = "expert"
WE = "weight"
GRID1 = ("arbitrary",)
QK = "qhd,khd->hqk"
QV = "hqk,khd->qhd"
KV = "hqk,qhd->khd"

norm_eps = 1e-05
rope_base = 10000.0


def rms_scale(values):
    return lax.rsqrt(jnp.mean(values * values, axis=-1, keepdims=True) + norm_eps)


def rope_tables(length, head_width):
    exponent = jnp.arange(head_width // 2).astype(F32) * 2.0 / head_width
    inverse = rope_base ** (-exponent)
    angles = jnp.arange(length).astype(F32)[:, None] * inverse[None, :]
    angles = jnp.concatenate([angles, angles], axis=-1)[:, None, :]
    return (jnp.cos(angles), jnp.sin(angles))


def rotate(values, cosine, sine_table):
    half_width = values.shape[-1] // 2
    turned = jnp.concatenate([-values[..., half_width:], values[..., :half_width]], axis=-1)
    return values * cosine + turned * sine_table


def rotate_back(values, cosine, sine_table):
    half_width = values.shape[-1] // 2
    shifted = values * sine_table
    turned = jnp.concatenate([shifted[..., half_width:], -shifted[..., :half_width]], axis=-1)
    return values * cosine + turned


def dot32(left, right):
    return jnp.dot(left, right, preferred_element_type=F32)


def ein(spec, left, right):
    return jnp.einsum(spec, left, right, preferred_element_type=F32)


def dot_nt(left, right):
    return lax.dot_general(left, right, NT, preferred_element_type=F32)


def swap(values, distance):
    count = lax.axis_size(EX)
    return lax.ppermute(values, EX, [(i, i ^ distance) for i in range(count)])


def swap_weight(values, distance):
    count = lax.axis_size(WE)
    return lax.ppermute(values, WE, [(i, i ^ distance) for i in range(count)])


def shift_weight(values, distance):
    count = lax.axis_size(WE)
    return lax.ppermute(values, WE, [(i, (i + distance) % count) for i in range(count)])


def gather_start(block):
    if lax.axis_size(EX) != 8:
        return ()
    return (swap(block, 2), swap(block, 4))


def gather_finish(block, near):
    count = lax.axis_size(EX)
    if count != 8:
        return [block] + [swap(block, r) for r in range(1, count)]
    half = block.shape[0] // 2
    from_x, from_y = near
    diagonal = jnp.concatenate([swap(from_y[:half], 2), swap(from_x[half:], 4)], axis=0)
    blocks = []
    for own in (block, from_x, from_y, diagonal):
        blocks += [own, swap(own, 1)]
    return blocks


def scatter_expert(parts):
    count = lax.axis_size(EX)
    if count != 8:
        total = parts[0].astype(F32)
        for r in range(1, count):
            total = total + swap(parts[r], r).astype(F32)
        return total
    sums = {r: parts[r].astype(F32) + swap(parts[r ^ 1], 1).astype(F32) for r in (6, 2, 4, 0)}
    half = sums[6].shape[0] // 2
    far = sums[6].astype(BF)
    over_x = swap(far[:half], 2).astype(F32)
    over_y = swap(far[half:], 4).astype(F32)
    to_y = jnp.concatenate([sums[4][:half] + over_x, sums[4][half:]], axis=0).astype(BF)
    to_x = jnp.concatenate([sums[2][:half], sums[2][half:] + over_y], axis=0).astype(BF)
    return sums[0] + swap(to_x, 2).astype(F32) + swap(to_y, 4).astype(F32)


def sum_weight_small(values):
    distance = 1
    while distance < lax.axis_size(WE):
        values = values + swap_weight(values, distance)
        distance = distance * 2
    return values


def scatter_weight(pick):
    own = pick(0).astype(F32)
    others = [shift_weight(pick(step).astype(BF), step) for step in range(1, lax.axis_size(WE))]
    return functools.reduce(lambda total, other: total + other.astype(F32), others, own)


def gather_weight_relative(block):
    blocks = [block]
    for step in range(1, lax.axis_size(WE)):
        blocks.append(shift_weight(block, -step))
    return jnp.concatenate(blocks, axis=0)


def gather_weight(block):
    count = lax.axis_size(WE)
    place = lax.axis_index(WE)
    rows = block.shape[0]
    whole = jnp.zeros((count * rows,) + block.shape[1:], block.dtype)
    whole = lax.dynamic_update_slice_in_dim(whole, block, place * rows, 0)
    for step in range(1, count):
        whole = lax.dynamic_update_slice_in_dim(
            whole, shift_weight(block, step), ((place - step) % count) * rows, 0
        )
    return whole


def two_parts(values):
    high = values.astype(BF)
    low = (values - high.astype(F32)).astype(BF)
    return high, low


def row_places(shape, axis, first_lane):
    row = lax.broadcasted_iota(jnp.int32, shape, axis)
    expert = (row * 683) >> 16
    return first_lane + expert, row - expert * CAP


def pick_matrix(table, local_experts, first_lane):
    rows = local_experts * CAP
    expert, _ = row_places((rows, EXTRA), 0, first_lane)
    lane = lax.broadcasted_iota(jnp.int32, (rows, EXTRA), 1)
    wanted = dot_nt((lane == expert).astype(BF), table)
    _, slot = row_places(wanted.shape, 0, first_lane)
    return (wanted == slot.astype(F32)).astype(BF)


def put_matrix(table, local_experts, first_lane):
    rows = local_experts * CAP
    expert, _ = row_places((EXTRA, rows), 1, first_lane)
    lane = lax.broadcasted_iota(jnp.int32, (EXTRA, rows), 0)
    wanted = dot32(table, (lane == expert).astype(BF))
    _, slot = row_places(wanted.shape, 1, first_lane)
    return (wanted == slot.astype(F32)).astype(BF)


def params():
    return pltpu.CompilerParams(dimension_semantics=GRID1, vmem_limit_bytes=VMEM_BYTES)


def prepare_kernel(grad_ref, slot_ref, out_ref):
    out_ref[:, :D] = grad_ref[...].astype(BF)
    out_ref[:, D:] = slot_ref[...]


def prepare_call(out_grad, slot_wide):
    length = out_grad.shape[0]
    rows = length // 4
    return pl.pallas_call(
        prepare_kernel,
        grid=(4,),
        in_specs=[pl.BlockSpec((rows, D), lambda i: (i, 0)), pl.BlockSpec((rows, EXTRA), lambda i: (i, 0))],
        out_specs=pl.BlockSpec((rows, WIDE), lambda i: (i, 0)),
        out_shape=jax.ShapeDtypeStruct((length, WIDE), BF),
        cost_estimate=pl.CostEstimate(
            flops=length * D, transcendentals=0, bytes_accessed=length * WIDE * 6
        ),
    )(out_grad, slot_wide)


def cotangent_kernel(seqs, local_experts, first_ref, *refs):
    cots = refs[:seqs]
    down_ref = refs[seqs]
    rows_ref, hidden_ref, held = refs[seqs + 1 :]
    e = pl.program_id(0)
    first = first_ref[0]

    @pl.when(e == 0)
    def _():
        for s in range(seqs):
            pick = pick_matrix(cots[s][:, D:], local_experts, first)
            held[s] = dot32(pick, cots[s][:, :D]).astype(BF)

    rows = held[:, pl.ds(pl.multiple_of(e * CAP, CAP), CAP), :]
    rows_ref[:, 0] = rows
    hidden_ref[:, 0] = dot_nt(rows.reshape(seqs * CAP, D), down_ref[0]).reshape(seqs, CAP, -1)


def cotangent_call(first, cots, down_weight):
    seqs = len(cots)
    local_experts, width, _ = down_weight.shape
    length = cots[0].shape[0]
    whole = pl.BlockSpec((length, WIDE), lambda e, f: (0, 0), pipeline_mode=pl.Buffered(1))
    return pl.pallas_call(
        functools.partial(cotangent_kernel, seqs, local_experts),
        grid_spec=pltpu.PrefetchScalarGridSpec(
            num_scalar_prefetch=1,
            grid=(local_experts,),
            in_specs=[whole] * seqs + [pl.BlockSpec((1, width, D), lambda e, f: (e, 0, 0))],
            out_specs=[
                pl.BlockSpec((seqs, 1, CAP, D), lambda e, f: (0, e, 0, 0)),
                pl.BlockSpec((seqs, 1, CAP, width), lambda e, f: (0, e, 0, 0)),
            ],
            scratch_shapes=[pltpu.VMEM((seqs, local_experts * CAP, D), BF)],
        ),
        out_shape=[
            jax.ShapeDtypeStruct((seqs, local_experts, CAP, D), BF),
            jax.ShapeDtypeStruct((seqs, local_experts, CAP, width), F32),
        ],
        compiler_params=params(),
        cost_estimate=pl.CostEstimate(
            flops=2 * seqs * local_experts * CAP * D * (length + width),
            transcendentals=0,
            bytes_accessed=seqs * (length * WIDE + local_experts * CAP * (D + 2 * width)) * 2
            + local_experts * width * D * 2,
        ),
    )(first, *cots, down_weight)


def expert_kernel(seqs, local_experts, extra, first_ref, *refs):
    tokens = refs[:seqs]
    tables = refs[seqs : 2 * seqs]
    grad_ref, gate_ref, up_ref, down_ref = refs[2 * seqs : 2 * seqs + 4]
    rest = refs[2 * seqs + 4 + extra :]
    rows_ref, hidden_ref, grad_gate_ref, grad_up_ref, out_ref = rest[:5]
    backs = rest[5 : 5 + seqs]
    held = rest[5 + seqs]
    e = pl.program_id(0)
    first = first_ref[0]
    count = seqs * CAP

    @pl.when(e == 0)
    def _():
        for s in range(seqs):
            pick = pick_matrix(tables[s][...], local_experts, first + EXPERTS)
            held[s] = dot32(pick, tokens[s][...]).astype(BF)

    span = pl.ds(pl.multiple_of(e * CAP, CAP), CAP)
    both = held[:, span, :].reshape(count, WIDE)
    rows = both[:, :D]
    rows_ref[:, 0] = rows.reshape(seqs, CAP, D)
    lane = lax.broadcasted_iota(jnp.int32, (count, EXTRA), 1)
    own_high = lane == first + e
    own_low = lane == first + e + EXPERTS
    gates = jnp.sum(
        jnp.where(own_high | own_low, both[:, D:].astype(F32), 0.0), axis=1, keepdims=True
    )
    gate_pre = dot32(rows, gate_ref[0])
    up_pre = dot32(rows, up_ref[0])
    grad_hidden = grad_ref[:, 0].reshape(count, -1)
    sigmoid_gate = jax.nn.sigmoid(gate_pre)
    silu_gate = gate_pre * sigmoid_gate
    hidden = silu_gate * up_pre
    gated = (gates * hidden).astype(BF)
    gate_grads = jnp.sum(hidden * grad_hidden, axis=1, keepdims=True)
    grad_hidden = gates * grad_hidden
    grad_gate = (
        grad_hidden * up_pre * sigmoid_gate * (1.0 + gate_pre * (1.0 - sigmoid_gate))
    ).astype(BF)
    grad_up = (grad_hidden * silu_gate).astype(BF)
    hidden_ref[:, 0] = gated.reshape(seqs, CAP, -1)
    grad_gate_ref[:, 0] = grad_gate.reshape(seqs, CAP, -1)
    grad_up_ref[:, 0] = grad_up.reshape(seqs, CAP, -1)
    out_ref[:, 0] = dot32(gated, down_ref[0]).astype(BF).reshape(seqs, CAP, D)
    back = dot_nt(grad_gate, gate_ref[0]) + dot_nt(grad_up, up_ref[0])
    held[:, span, :D] = back.astype(BF).reshape(seqs, CAP, D)
    high = gate_grads.astype(BF).astype(F32)
    spread = jnp.where(own_high, high, jnp.where(own_low, gate_grads - high, 0.0))
    held[:, span, D:] = spread.astype(BF).reshape(seqs, CAP, EXTRA)

    @pl.when(e == local_experts - 1)
    def _():
        for s in range(seqs):
            put = put_matrix(tables[s][...], local_experts, first + EXPERTS)
            backs[s][...] = dot32(put, held[s]).astype(BF)


def expert_call(first, tokens, cots, grads, part, gate_weight, up_weight, down_weight, after):
    seqs = len(tokens)
    local_experts, width, _ = down_weight.shape
    length = tokens[0].shape[0]
    rows = local_experts * CAP
    once = pl.Buffered(1)
    per_expert = lambda last, part=0: pl.BlockSpec((seqs, 1, CAP, last), lambda e, f: (part, e, 0, 0))
    packed = lambda last: jax.ShapeDtypeStruct((seqs, local_experts, CAP, last), BF)
    return pl.pallas_call(
        functools.partial(expert_kernel, seqs, local_experts, len(after)),
        grid_spec=pltpu.PrefetchScalarGridSpec(
            num_scalar_prefetch=1,
            grid=(local_experts,),
            in_specs=[pl.BlockSpec((length, WIDE), lambda e, f: (0, 0), pipeline_mode=once)] * seqs
            + [pl.BlockSpec((length, EXTRA), lambda e, f: (0, D // EXTRA), pipeline_mode=once)] * seqs
            + [
                per_expert(width, part),
                pl.BlockSpec((1, D, width), lambda e, f: (e, 0, 0)),
                pl.BlockSpec((1, D, width), lambda e, f: (e, 0, 0)),
                pl.BlockSpec((1, width, D), lambda e, f: (e, 0, 0)),
            ]
            + [pl.BlockSpec(memory_space=pl.ANY)] * len(after),
            out_specs=[per_expert(last) for last in (D, width, width, width, D)]
            + [pl.BlockSpec((length, WIDE), lambda e, f: (0, 0), pipeline_mode=once)] * seqs,
            scratch_shapes=[pltpu.VMEM((seqs, rows, WIDE), BF)],
        ),
        out_shape=[packed(last) for last in (D, width, width, width, D)]
        + [jax.ShapeDtypeStruct((length, WIDE), BF)] * seqs,
        compiler_params=params(),
        cost_estimate=pl.CostEstimate(
            flops=2 * seqs * rows * D * (2 * length + 5 * width),
            transcendentals=seqs * rows * width,
            bytes_accessed=seqs * (2 * length * WIDE + rows * (2 * D + 5 * width)) * 2
            + 3 * local_experts * width * D * 2,
        ),
    )(first, *tokens, *cots, grads, gate_weight, up_weight, down_weight, *after)


def mixture_kernel(seqs, local_experts, first_ref, rows_ref, *refs):
    tables, outs, put = refs[:seqs], refs[seqs : 2 * seqs], refs[2 * seqs]
    first = first_ref[0]

    @pl.when(pl.program_id(0) == 0)
    def _():
        for s in range(seqs):
            put[s] = put_matrix(tables[s][...], local_experts, first)

    for s in range(seqs):
        outs[s][...] = dot32(put[s], rows_ref[s].reshape(local_experts * CAP, -1)).astype(BF)


def mixture_call(first, out_rows, cots):
    seqs, local_experts = out_rows.shape[:2]
    length = cots[0].shape[0]
    columns = D // 4
    rows = local_experts * CAP
    return pl.pallas_call(
        functools.partial(mixture_kernel, seqs, local_experts),
        grid_spec=pltpu.PrefetchScalarGridSpec(
            num_scalar_prefetch=1,
            grid=(4,),
            in_specs=[pl.BlockSpec((seqs, local_experts, CAP, columns), lambda c, f: (0, 0, 0, c))]
            + [pl.BlockSpec((length, EXTRA), lambda c, f: (0, D // EXTRA))] * seqs,
            out_specs=[pl.BlockSpec((length, columns), lambda c, f: (0, c))] * seqs,
            scratch_shapes=[pltpu.VMEM((seqs, length, rows), BF)],
        ),
        out_shape=[jax.ShapeDtypeStruct((length, D), BF)] * seqs,
        compiler_params=params(),
        cost_estimate=pl.CostEstimate(
            flops=2 * seqs * rows * length * D,
            transcendentals=0,
            bytes_accessed=seqs * (rows + length) * D * 2,
        ),
    )(first, out_rows, *cots)


def weight_grad_kernel(parts, *refs):
    ins, (gate_ref, up_ref, down_ref), (rows, cots, small) = (
        refs[: 5 * parts],
        refs[5 * parts : 5 * parts + 3],
        refs[5 * parts + 3 :],
    )
    width = gate_ref.shape[2]
    for p in range(parts):
        rows_ref, cot_ref, hidden_ref, grad_gate_ref, grad_up_ref = ins[5 * p : 5 * p + 5]
        count = rows_ref.shape[0] * CAP
        span = pl.ds(p * count, count)
        rows[span] = rows_ref[:, 0].reshape(count, D)
        cots[span] = cot_ref[:, 0].reshape(count, D)
        small[span, :width] = grad_gate_ref[:, 0].reshape(count, width)
        small[span, width : 2 * width] = grad_up_ref[:, 0].reshape(count, width)
        small[span, 2 * width :] = hidden_ref[:, 0].reshape(count, width)
    both = dot32(rows[...].T, small[:, : 2 * width])
    gate_ref[0] = both[:, :width]
    up_ref[0] = both[:, width:]
    down_ref[0] = dot32(small[:, 2 * width :].T, cots[...])


def weight_grads(pieces, parts):
    seqs, local_experts, _, width = pieces[0][2].shape
    if lax.axis_size(EX) != 8:
        rows, cots, hidden, grad_gate, grad_up = (
            jnp.concatenate([piece[i] for piece in pieces], axis=0) for i in range(5)
        )
        return (
            ein("secd,secf->edf", rows, grad_gate),
            ein("secd,secf->edf", rows, grad_up),
            ein("secf,secd->efd", hidden, cots),
        )
    total = len(pieces) * seqs * CAP
    block = lambda last, part=0: pl.BlockSpec((seqs, 1, CAP, last), lambda e: (part, e, 0, 0))
    specs = []
    for part in parts:
        specs += [block(D), block(D, part), block(width), block(width), block(width)]
    flat = [array for piece in pieces for array in piece]
    return pl.pallas_call(
        functools.partial(weight_grad_kernel, len(pieces)),
        grid=(local_experts,),
        in_specs=specs,
        out_specs=[
            pl.BlockSpec((1, D, width), lambda e: (e, 0, 0)),
            pl.BlockSpec((1, D, width), lambda e: (e, 0, 0)),
            pl.BlockSpec((1, width, D), lambda e: (e, 0, 0)),
        ],
        out_shape=[
            jax.ShapeDtypeStruct((local_experts, D, width), F32),
            jax.ShapeDtypeStruct((local_experts, D, width), F32),
            jax.ShapeDtypeStruct((local_experts, width, D), F32),
        ],
        scratch_shapes=[
            pltpu.VMEM((total, D), BF),
            pltpu.VMEM((total, D), BF),
            pltpu.VMEM((total, 3 * width), BF),
        ],
        compiler_params=params(),
        cost_estimate=pl.CostEstimate(
            flops=6 * local_experts * total * D * width,
            transcendentals=0,
            bytes_accessed=local_experts * (total * (2 * D + 3 * width) * 2 + 3 * D * width * 4),
        ),
    )(*flat)


def dense_grad_kernel(pairs, tail, owner_ref, *refs):
    lefts, rights = refs[:pairs], refs[pairs : 2 * pairs]
    outs = refs[2 * pairs + tail :]
    rows = D // len(outs)
    for r, out in enumerate(outs):
        span = pl.ds(pl.multiple_of((owner_ref[0] ^ r) * rows, rows), rows)
        column = 0
        for left, right in zip(lefts, rights, strict=True):
            width = right.shape[0]
            turned = left[:, span].T
            out[:rows, column : column + width] = dot_nt(turned, right[...]).astype(BF)
            column = column + width
        if tail:
            out[rows:, :rows] = refs[2 * pairs][:, span]
            out[rows:, rows:] = jnp.zeros((TAIL, column - rows), BF)


def dense_grads(owner, lefts, rights, small=None):
    owners = lax.axis_size(EX)
    rows = D // owners
    width = sum(right.shape[1] for right in rights)
    tail = 0 if small is None else 1
    if owners != 8:
        full = jnp.concatenate(
            [dot32(left[:, :D].T, right) for left, right in zip(lefts, rights, strict=True)], axis=1
        )
        full = full.astype(BF).reshape(owners, rows, width)
        if tail:
            below = jnp.moveaxis(small.reshape(TAIL, owners, rows), 1, 0)
            below = jnp.pad(below, ((0, 0), (0, 0), (0, width - rows)))
            full = jnp.concatenate([full, below], axis=1)
        return [lax.dynamic_index_in_dim(full, owner ^ r, 0, keepdims=False) for r in range(owners)]
    length = lefts[0].shape[0]
    out_rows = rows + TAIL * tail
    vmem = pl.BlockSpec(memory_space=pltpu.VMEM)
    operands = [*lefts, *[right.T for right in rights]] + ([small] if tail else [])
    return pl.pallas_call(
        functools.partial(dense_grad_kernel, len(lefts), tail),
        in_specs=[pl.BlockSpec(memory_space=pltpu.SMEM)] + [vmem] * len(operands),
        out_specs=[vmem] * owners,
        out_shape=[jax.ShapeDtypeStruct((out_rows, width), BF)] * owners,
        compiler_params=pltpu.CompilerParams(vmem_limit_bytes=VMEM_BYTES),
        cost_estimate=pl.CostEstimate(
            flops=2 * length * D * width,
            transcendentals=0,
            bytes_accessed=(len(lefts) * length * D + length * width + D * width) * 2,
        ),
    )(jnp.full((1,), owner, jnp.int32), *operands)


def layer(
    block_input,
    out_grad,
    norm_one,
    query_weight,
    key_weight,
    value_weight,
    query_gain,
    key_gain,
    output_weight,
    norm_two,
    router_weight,
    gate_weight,
    up_weight,
    down_weight,
    segment_ids,
    expert_routes,
    expert_slots,
):
    length = block_input.shape[0]
    local_width = query_weight.shape[1]
    head_count = local_width // HD
    score_scale = HD ** (-0.5)
    groups = lax.axis_size(WE)
    place = lax.axis_index(WE)
    owners = lax.axis_size(EX)
    owner = lax.axis_index(EX)
    local_experts = gate_weight.shape[0]
    first_expert = owner * local_experts
    quarter = length // groups
    col_width = D // groups
    first_row = place * quarter

    chosen = expert_routes[:, :, None] == jnp.arange(EXPERTS)[None, None, :]
    slot_table = jnp.min(jnp.where(chosen, expert_slots[:, :, None], CAP), axis=1).astype(BF)
    slot_turned = lax.dynamic_slice_in_dim(
        jnp.concatenate([slot_table, slot_table], axis=0), first_row, length, 0
    )
    slot_wide = jnp.concatenate([slot_table, slot_turned], axis=1)

    inputs = block_input.astype(F32)
    scale_one = rms_scale(inputs)
    normed_one = (inputs * scale_one * norm_one).astype(BF)
    query_pre = dot32(normed_one, query_weight)
    key_pre = dot32(normed_one, key_weight)
    squares = jnp.stack(
        [jnp.sum(query_pre * query_pre, axis=-1), jnp.sum(key_pre * key_pre, axis=-1)]
    )
    squares = sum_weight_small(squares)
    cotangent = prepare_call(out_grad, slot_wide)
    cotangents_near = gather_start(cotangent)
    value_flat = dot32(normed_one, value_weight).astype(BF)
    query_scale = lax.rsqrt(squares[0] / D + norm_eps)[:, None]
    key_scale = lax.rsqrt(squares[1] / D + norm_eps)[:, None]
    query_gains = query_gain.reshape(-1)
    key_gains = key_gain.reshape(-1)
    head_shape = (length, head_count, HD)
    cosine, sine_table = rope_tables(length, HD)
    query_rot = rotate(
        (query_pre * query_scale * query_gains).reshape(head_shape), cosine, sine_table
    ).astype(BF)
    key_rot = rotate(
        (key_pre * key_scale * key_gains).reshape(head_shape), cosine, sine_table
    ).astype(BF)
    value_heads = value_flat.reshape(head_shape)
    segment_row = segment_ids[0]
    positions = jnp.arange(length)
    allowed = (positions[:, None] >= positions[None, :]) & (
        segment_row[:, None] == segment_row[None, :]
    )
    scores = jnp.where(allowed[None], ein(QK, query_rot, key_rot) * score_scale, -1e30)
    highest = jnp.max(scores, axis=-1, keepdims=True)
    exponent = jnp.exp(scores - highest)
    denominator = jnp.sum(exponent, axis=-1, keepdims=True)
    soft = exponent / denominator
    soft_b = soft.astype(BF)
    attended = ein(QV, soft_b, value_heads).reshape(length, local_width).astype(BF)
    attention_part = dot32(attended, output_weight).astype(BF)
    cotangents = gather_finish(cotangent, cotangents_near)

    input_rows = lax.dynamic_slice_in_dim(block_input, first_row, quarter, 0).astype(F32)
    second = input_rows + scatter_weight(
        lambda step: lax.dynamic_slice_in_dim(
            attention_part, ((place + step) % groups) * quarter, quarter, 0
        ),
    )
    scale_two = rms_scale(second)
    normed_rows = (second * scale_two * norm_two).astype(BF)
    gate_rows = jax.nn.softmax(dot32(normed_rows, router_weight), axis=-1)
    token_rows = jnp.concatenate([normed_rows, *two_parts(gate_rows)], axis=1)
    tokens_own = gather_weight_relative(token_rows)
    tokens = gather_finish(tokens_own, gather_start(tokens_own))

    first_array = jnp.full((1,), first_expert, jnp.int32)
    pairs = [(r, r + 1) for r in range(0, owners, 2)]
    cot_groups = pairs
    if owners == 8:
        pairs = [(0, 1), (2, 3), (6, 7), (4, 5)]
        cot_groups = [(0, 1), (2, 3), (4, 5, 6, 7)]
    cot_rows = {}
    for group in cot_groups:
        both = cotangent_call(first_array, [cotangents[r] for r in group], down_weight)
        for i in range(0, len(group), 2):
            cot_rows[group[i]] = (*both, i // 2)
    after, back, pieces, parts, out_rows = [], {}, [], [], {}
    for pair in pairs:
        rows_grad, grad_hidden, part = cot_rows[pair[0]]
        rows_in, hidden, grad_gate, grad_up, out_rows[pair], *backs = expert_call(
            first_array,
            [tokens[r] for r in pair],
            [cotangents[r] for r in pair],
            grad_hidden,
            part,
            gate_weight,
            up_weight,
            down_weight,
            after,
        )
        after = [hidden]
        pieces.append((rows_in, rows_grad, hidden, grad_gate, grad_up))
        parts.append(part)
        back.update(zip(pair, backs, strict=True))
    gate_result, up_result, down_result = weight_grads(pieces, parts)
    back_own = scatter_expert([back[r] for r in range(owners)])
    back_rows = scatter_weight(lambda step: back_own[step * quarter : (step + 1) * quarter])

    mixed_out = {}
    for pair in [(6, 7), (0, 1), (2, 3), (4, 5)] if owners == 8 else pairs:
        outs = mixture_call(first_array, out_rows[pair], [cotangents[r] for r in pair])
        mixed_out.update(zip(pair, outs, strict=True))
    own_rows = lax.dynamic_slice_in_dim(mixed_out[0], first_row, quarter, 0).astype(F32) + second
    mixed_out[0] = lax.dynamic_update_slice_in_dim(mixed_out[0], own_rows.astype(BF), first_row, 0)
    mixture_own = scatter_expert([mixed_out[r] for r in range(owners)])
    block_output = scatter_weight(
        lambda step: lax.dynamic_slice_in_dim(
            mixture_own, ((place + step) % groups) * col_width, col_width, 1
        ),
    )

    grad_probs = back_rows[:, D : D + EXPERTS] + back_rows[:, D + EXPERTS :]
    grad_logits = gate_rows * (grad_probs - jnp.sum(gate_rows * grad_probs, axis=-1, keepdims=True))
    grad_logits_b = grad_logits.astype(BF)
    grad_normed_two = back_rows[:, :D] + dot32(grad_logits_b, router_weight.T)
    weighted_two = grad_normed_two * norm_two
    norm_two_part = sum_weight_small(jnp.sum(grad_normed_two * second * scale_two, axis=0))
    out_grad_rows = lax.dynamic_slice_in_dim(out_grad, first_row, quarter, 0)
    grad_second = (
        out_grad_rows
        + scale_two * weighted_two
        - second * scale_two**3 * jnp.mean(second * weighted_two, axis=-1, keepdims=True)
    )
    second_rows = jnp.concatenate(
        [grad_second.astype(BF), grad_logits_b, jnp.zeros((quarter, EXTRA - EXPERTS), BF)], axis=1
    )
    second_all = gather_weight(second_rows)
    grad_second_b = second_all[:, :D]

    grad_mixed = dot_nt(grad_second_b, output_weight).astype(BF).reshape(head_shape)
    grad_soft = ein(QK, grad_mixed, value_heads)
    inner = jnp.sum(soft * grad_soft, axis=-1, keepdims=True)
    grad_scores = (soft * (grad_soft - inner)).astype(BF)
    grad_query_rot = ein(QV, grad_scores, key_rot) * score_scale
    grad_key_rot = ein(KV, grad_scores, query_rot) * score_scale
    grad_values_b = ein(KV, soft_b, grad_mixed).reshape(length, local_width).astype(BF)
    grad_query_norm = rotate_back(grad_query_rot, cosine, sine_table).reshape(length, local_width)
    grad_key_norm = rotate_back(grad_key_rot, cosine, sine_table).reshape(length, local_width)
    weighted_query = grad_query_norm * query_gains
    weighted_key = grad_key_norm * key_gains
    query_gain_part = jnp.sum(grad_query_norm * query_pre * query_scale, axis=0)
    key_gain_part = jnp.sum(grad_key_norm * key_pre * key_scale, axis=0)
    cross = jnp.stack(
        [jnp.sum(query_pre * weighted_query, axis=-1), jnp.sum(key_pre * weighted_key, axis=-1)]
    )
    cross = sum_weight_small(cross)
    sums_a = dense_grads(owner, [normed_one, second_all], [grad_values_b, attended])
    reduced_a = scatter_expert(sums_a)
    grad_query_pre = (
        query_scale * weighted_query - query_pre * query_scale**3 * (cross[0] / D)[:, None]
    ).astype(BF)
    grad_key_pre = (
        key_scale * weighted_key - key_pre * key_scale**3 * (cross[1] / D)[:, None]
    ).astype(BF)
    grad_normed_local = (
        dot_nt(grad_query_pre, query_weight)
        + dot_nt(grad_key_pre, key_weight)
        + dot_nt(grad_values_b, value_weight)
    )
    inputs_again = lax.optimization_barrier(block_input).astype(F32)
    norm_one_part = jnp.sum(grad_normed_local * inputs_again * scale_one, axis=0)
    grad_normed_one = scatter_weight(
        lambda step: lax.dynamic_slice_in_dim(
            grad_normed_local, ((place + step) % groups) * quarter, quarter, 0
        ),
    )
    scale_rows = lax.dynamic_slice_in_dim(scale_one, first_row, quarter, 0)
    weighted_one = grad_normed_one * norm_one
    input_result = (
        grad_second
        + scale_rows * weighted_one
        - input_rows * scale_rows**3 * jnp.mean(input_rows * weighted_one, axis=-1, keepdims=True)
    )

    router_cols = EXPERTS // groups
    logits_mine = lax.dynamic_slice_in_dim(second_all, D + place * router_cols, router_cols, 1)
    tokens_turned = lax.dynamic_slice_in_dim(
        jnp.concatenate([logits_mine, logits_mine], axis=0), first_row, length, 0
    )
    router_part = lax.dot_general(
        tokens_turned, tokens_own[:, :D], (((0,), (0,)), ((), ())), preferred_element_type=F32
    )
    rows = D // owners
    gain_width = HD // owners
    gains = jnp.concatenate([query_gain_part, key_gain_part]).reshape(2 * head_count, owners, gain_width)
    gains = jnp.pad(gains, ((0, 0), (0, 0), (0, rows - gain_width))).reshape(2 * head_count, D)
    small = jnp.concatenate([router_part, norm_one_part[None], norm_two_part[None], gains], axis=0)
    small = jnp.pad(small, ((0, TAIL - small.shape[0]), (0, 0))).astype(BF)
    sums_b = dense_grads(owner, [normed_one, normed_one], [grad_query_pre, grad_key_pre], small)
    reduced_b = scatter_expert(sums_b)
    tail = reduced_b[rows:, :rows]
    norm_one_result = sum_weight_small(tail[router_cols])
    gain_result = tail[router_cols + 2 : router_cols + 2 + 2 * head_count, :gain_width]
    width = local_width
    return (
        block_output,
        input_result,
        norm_one_result,
        reduced_b[:rows, :width],
        reduced_b[:rows, width:],
        reduced_a[:, :width],
        gain_result[:head_count],
        gain_result[head_count:],
        reduced_a[:, width:].T,
        tail[router_cols + 1],
        tail[:router_cols].T,
        gate_result,
        up_result,
        down_result,
    )


def solution(mesh):
    rows = P(EX, None)
    columns = P(None, WE)
    heads = P(WE, None)
    mixed = P(EX, None, WE)
    down = P(EX, WE, None)
    in_specs = (
        (rows, rows, P(), columns, columns, columns, heads, heads, heads)
        + (P(), P(), mixed, mixed, down, rows, rows, rows)
    )
    square = P(EX, WE)
    turned = P(WE, EX)
    out_specs = (
        (square, P((EX, WE), None), P(EX), square, square, square)
        + (turned, turned, turned, P(EX), square, mixed, mixed, down)
    )
    return jax.shard_map(layer, mesh=mesh, in_specs=in_specs, out_specs=out_specs, check_vma=False)
```

```python
import functools

import jax
import jax.numpy as jnp
from jax import lax
from jax.experimental import pallas as pl
from jax.experimental.pallas import tpu as pltpu
from jax.sharding import PartitionSpec as P

D = 2048
HD = 128
EXPERTS = 64
CAP = 96
EXTRA = 128
WIDE = D + EXTRA
TAIL = 32
BF = jnp.bfloat16
F32 = jnp.float32
NT = (((1,), (1,)), ((), ()))
VMEM_BYTES = 67_000_000
EX = "expert"
WE = "weight"
GRID1 = ("arbitrary",)
QK = "qhd,khd->hqk"
QV = "hqk,khd->qhd"
KV = "hqk,qhd->khd"

norm_eps = 1e-05
rope_base = 10000.0


def rms_scale(values):
    return lax.rsqrt(jnp.mean(values * values, axis=-1, keepdims=True) + norm_eps)


def rope_tables(length, head_width):
    exponent = jnp.arange(head_width // 2).astype(F32) * 2.0 / head_width
    inverse = rope_base ** (-exponent)
    angles = jnp.arange(length).astype(F32)[:, None] * inverse[None, :]
    angles = jnp.concatenate([angles, angles], axis=-1)[:, None, :]
    return (jnp.cos(angles), jnp.sin(angles))


def rotate(values, cosine, sine_table):
    half_width = values.shape[-1] // 2
    turned = jnp.concatenate([-values[..., half_width:], values[..., :half_width]], axis=-1)
    return values * cosine + turned * sine_table


def rotate_back(values, cosine, sine_table):
    half_width = values.shape[-1] // 2
    shifted = values * sine_table
    turned = jnp.concatenate([shifted[..., half_width:], -shifted[..., :half_width]], axis=-1)
    return values * cosine + turned


def dot32(left, right):
    return jnp.dot(left, right, preferred_element_type=F32)


def ein(spec, left, right):
    return jnp.einsum(spec, left, right, preferred_element_type=F32)


def dot_nt(left, right):
    return lax.dot_general(left, right, NT, preferred_element_type=F32)


def swap(values, distance):
    count = lax.axis_size(EX)
    return lax.ppermute(values, EX, [(i, i ^ distance) for i in range(count)])


def swap_weight(values, distance):
    count = lax.axis_size(WE)
    return lax.ppermute(values, WE, [(i, i ^ distance) for i in range(count)])


def shift_weight(values, distance):
    count = lax.axis_size(WE)
    return lax.ppermute(values, WE, [(i, (i + distance) % count) for i in range(count)])


def gather_start(block):
    if lax.axis_size(EX) != 8:
        return ()
    return (swap(block, 2), swap(block, 4))


def gather_finish(block, near):
    count = lax.axis_size(EX)
    if count != 8:
        return [block] + [swap(block, r) for r in range(1, count)]
    half = block.shape[0] // 2
    from_x, from_y = near
    diagonal = jnp.concatenate([swap(from_y[:half], 2), swap(from_x[half:], 4)], axis=0)
    blocks = []
    for own in (block, from_x, from_y, diagonal):
        blocks += [own, swap(own, 1)]
    return blocks


def scatter_expert(parts, cut=0):
    count = lax.axis_size(EX)
    if count != 8:
        total = parts[0].astype(F32)
        for r in range(1, count):
            total = total + swap(parts[r], r).astype(F32)
        return (total[:, :cut], total[:, cut:]) if cut else total
    sums = {r: parts[r].astype(F32) + swap(parts[r ^ 1], 1).astype(F32) for r in (6, 2, 4, 0)}
    half = sums[6].shape[0] // 2
    far = sums[6].astype(BF)
    over_x = swap(far[:half], 2).astype(F32)
    over_y = swap(far[half:], 4).astype(F32)
    to_y = jnp.concatenate([sums[4][:half] + over_x, sums[4][half:]], axis=0).astype(BF)
    to_x = jnp.concatenate([sums[2][:half], sums[2][half:] + over_y], axis=0).astype(BF)
    if cut == 0:
        return sums[0] + swap(to_x, 2).astype(F32) + swap(to_y, 4).astype(F32)
    return tuple(
        sums[0][:, span]
        + swap(to_x[:, span], 2).astype(F32)
        + swap(to_y[:, span], 4).astype(F32)
        for span in (slice(0, cut), slice(cut, None))
    )


def sum_weight_small(values):
    distance = 1
    while distance < lax.axis_size(WE):
        values = values + swap_weight(values, distance)
        distance = distance * 2
    return values


def scatter_weight(pick):
    own = pick(0).astype(F32)
    others = [shift_weight(pick(step).astype(BF), step) for step in range(1, lax.axis_size(WE))]
    return functools.reduce(lambda total, other: total + other.astype(F32), others, own)


def gather_weight_relative(block):
    blocks = [block]
    for step in range(1, lax.axis_size(WE)):
        blocks.append(shift_weight(block, -step))
    return jnp.concatenate(blocks, axis=0)


def gather_weight(block):
    count = lax.axis_size(WE)
    place = lax.axis_index(WE)
    rows = block.shape[0]
    whole = jnp.zeros((count * rows,) + block.shape[1:], block.dtype)
    whole = lax.dynamic_update_slice_in_dim(whole, block, place * rows, 0)
    for step in range(1, count):
        whole = lax.dynamic_update_slice_in_dim(
            whole, shift_weight(block, step), ((place - step) % count) * rows, 0
        )
    return whole


def two_parts(values):
    high = values.astype(BF)
    low = (values - high.astype(F32)).astype(BF)
    return high, low


def row_places(shape, axis, first_lane):
    row = lax.broadcasted_iota(jnp.int32, shape, axis)
    expert = (row * 683) >> 16
    return first_lane + expert, row - expert * CAP


def pick_matrix(table, local_experts, first_lane):
    rows = local_experts * CAP
    expert, _ = row_places((rows, EXTRA), 0, first_lane)
    lane = lax.broadcasted_iota(jnp.int32, (rows, EXTRA), 1)
    wanted = dot_nt((lane == expert).astype(BF), table)
    _, slot = row_places(wanted.shape, 0, first_lane)
    return (wanted == slot.astype(F32)).astype(BF)


def put_matrix(table, local_experts, first_lane):
    rows = local_experts * CAP
    expert, _ = row_places((EXTRA, rows), 1, first_lane)
    lane = lax.broadcasted_iota(jnp.int32, (EXTRA, rows), 0)
    wanted = dot32(table, (lane == expert).astype(BF))
    _, slot = row_places(wanted.shape, 1, first_lane)
    return (wanted == slot.astype(F32)).astype(BF)


def params():
    return pltpu.CompilerParams(dimension_semantics=GRID1, vmem_limit_bytes=VMEM_BYTES)


def prepare_kernel(grad_ref, slot_ref, out_ref):
    out_ref[:, :D] = grad_ref[...].astype(BF)
    out_ref[:, D:] = slot_ref[...]


def prepare_call(out_grad, slot_wide):
    length = out_grad.shape[0]
    rows = length // 4
    return pl.pallas_call(
        prepare_kernel,
        grid=(4,),
        in_specs=[pl.BlockSpec((rows, D), lambda i: (i, 0)), pl.BlockSpec((rows, EXTRA), lambda i: (i, 0))],
        out_specs=pl.BlockSpec((rows, WIDE), lambda i: (i, 0)),
        out_shape=jax.ShapeDtypeStruct((length, WIDE), BF),
        cost_estimate=pl.CostEstimate(
            flops=length * D, transcendentals=0, bytes_accessed=length * WIDE * 6
        ),
    )(out_grad, slot_wide)


def cotangent_kernel(seqs, local_experts, first_ref, *refs):
    cots = refs[:seqs]
    down_ref = refs[seqs]
    rows_ref, hidden_ref, held = refs[seqs + 1 :]
    e = pl.program_id(0)
    first = first_ref[0]

    @pl.when(e == 0)
    def _():
        for s in range(seqs):
            pick = pick_matrix(cots[s][:, D:], local_experts, first)
            held[s] = dot32(pick, cots[s][:, :D]).astype(BF)

    rows = held[:, pl.ds(pl.multiple_of(e * CAP, CAP), CAP), :]
    rows_ref[:, 0] = rows
    hidden_ref[:, 0] = dot_nt(rows.reshape(seqs * CAP, D), down_ref[0]).reshape(seqs, CAP, -1)


def cotangent_call(first, cots, down_weight):
    seqs = len(cots)
    local_experts, width, _ = down_weight.shape
    length = cots[0].shape[0]
    whole = pl.BlockSpec((length, WIDE), lambda e, f: (0, 0), pipeline_mode=pl.Buffered(1))
    return pl.pallas_call(
        functools.partial(cotangent_kernel, seqs, local_experts),
        grid_spec=pltpu.PrefetchScalarGridSpec(
            num_scalar_prefetch=1,
            grid=(local_experts,),
            in_specs=[whole] * seqs + [pl.BlockSpec((1, width, D), lambda e, f: (e, 0, 0))],
            out_specs=[
                pl.BlockSpec((seqs, 1, CAP, D), lambda e, f: (0, e, 0, 0)),
                pl.BlockSpec((seqs, 1, CAP, width), lambda e, f: (0, e, 0, 0)),
            ],
            scratch_shapes=[pltpu.VMEM((seqs, local_experts * CAP, D), BF)],
        ),
        out_shape=[
            jax.ShapeDtypeStruct((seqs, local_experts, CAP, D), BF),
            jax.ShapeDtypeStruct((seqs, local_experts, CAP, width), F32),
        ],
        compiler_params=params(),
        cost_estimate=pl.CostEstimate(
            flops=2 * seqs * local_experts * CAP * D * (length + width),
            transcendentals=0,
            bytes_accessed=seqs * (length * WIDE + local_experts * CAP * (D + 2 * width)) * 2
            + local_experts * width * D * 2,
        ),
    )(first, *cots, down_weight)


def expert_kernel(seqs, local_experts, extra, first_ref, *refs):
    tokens = refs[:seqs]
    tables = refs[seqs : 2 * seqs]
    grad_ref, gate_ref, up_ref, down_ref = refs[2 * seqs : 2 * seqs + 4]
    rest = refs[2 * seqs + 4 + extra :]
    rows_ref, hidden_ref, grad_gate_ref, grad_up_ref, out_ref = rest[:5]
    backs = rest[5 : 5 + seqs]
    held = rest[5 + seqs]
    e = pl.program_id(0)
    first = first_ref[0]
    count = seqs * CAP

    @pl.when(e == 0)
    def _():
        for s in range(seqs):
            pick = pick_matrix(tables[s][...], local_experts, first + EXPERTS)
            held[s] = dot32(pick, tokens[s][...]).astype(BF)

    span = pl.ds(pl.multiple_of(e * CAP, CAP), CAP)
    both = held[:, span, :].reshape(count, WIDE)
    rows = both[:, :D]
    rows_ref[:, 0] = rows.reshape(seqs, CAP, D)
    lane = lax.broadcasted_iota(jnp.int32, (count, EXTRA), 1)
    own_high = lane == first + e
    own_low = lane == first + e + EXPERTS
    gates = jnp.sum(
        jnp.where(own_high | own_low, both[:, D:].astype(F32), 0.0), axis=1, keepdims=True
    )
    gate_pre = dot32(rows, gate_ref[0])
    up_pre = dot32(rows, up_ref[0])
    grad_hidden = grad_ref[:, 0].reshape(count, -1)
    sigmoid_gate = jax.nn.sigmoid(gate_pre)
    silu_gate = gate_pre * sigmoid_gate
    hidden = silu_gate * up_pre
    gated = (gates * hidden).astype(BF)
    gate_grads = jnp.sum(hidden * grad_hidden, axis=1, keepdims=True)
    grad_hidden = gates * grad_hidden
    grad_gate = (
        grad_hidden * up_pre * sigmoid_gate * (1.0 + gate_pre * (1.0 - sigmoid_gate))
    ).astype(BF)
    grad_up = (grad_hidden * silu_gate).astype(BF)
    hidden_ref[:, 0] = gated.reshape(seqs, CAP, -1)
    grad_gate_ref[:, 0] = grad_gate.reshape(seqs, CAP, -1)
    grad_up_ref[:, 0] = grad_up.reshape(seqs, CAP, -1)
    out_ref[:, 0] = dot32(gated, down_ref[0]).astype(BF).reshape(seqs, CAP, D)
    back = dot_nt(grad_gate, gate_ref[0]) + dot_nt(grad_up, up_ref[0])
    held[:, span, :D] = back.astype(BF).reshape(seqs, CAP, D)
    high = gate_grads.astype(BF).astype(F32)
    spread = jnp.where(own_high, high, jnp.where(own_low, gate_grads - high, 0.0))
    held[:, span, D:] = spread.astype(BF).reshape(seqs, CAP, EXTRA)

    @pl.when(e == local_experts - 1)
    def _():
        for s in range(seqs):
            put = put_matrix(tables[s][...], local_experts, first + EXPERTS)
            backs[s][...] = dot32(put, held[s]).astype(BF)


def expert_call(first, tokens, cots, grads, part, gate_weight, up_weight, down_weight, after):
    seqs = len(tokens)
    local_experts, width, _ = down_weight.shape
    length = tokens[0].shape[0]
    rows = local_experts * CAP
    once = pl.Buffered(1)
    per_expert = lambda last, part=0: pl.BlockSpec((seqs, 1, CAP, last), lambda e, f: (part, e, 0, 0))
    packed = lambda last: jax.ShapeDtypeStruct((seqs, local_experts, CAP, last), BF)
    return pl.pallas_call(
        functools.partial(expert_kernel, seqs, local_experts, len(after)),
        grid_spec=pltpu.PrefetchScalarGridSpec(
            num_scalar_prefetch=1,
            grid=(local_experts,),
            in_specs=[pl.BlockSpec((length, WIDE), lambda e, f: (0, 0), pipeline_mode=once)] * seqs
            + [pl.BlockSpec((length, EXTRA), lambda e, f: (0, D // EXTRA), pipeline_mode=once)] * seqs
            + [
                per_expert(width, part),
                pl.BlockSpec((1, D, width), lambda e, f: (e, 0, 0)),
                pl.BlockSpec((1, D, width), lambda e, f: (e, 0, 0)),
                pl.BlockSpec((1, width, D), lambda e, f: (e, 0, 0)),
            ]
            + [pl.BlockSpec(memory_space=pl.ANY)] * len(after),
            out_specs=[per_expert(last) for last in (D, width, width, width, D)]
            + [pl.BlockSpec((length, WIDE), lambda e, f: (0, 0), pipeline_mode=once)] * seqs,
            scratch_shapes=[pltpu.VMEM((seqs, rows, WIDE), BF)],
        ),
        out_shape=[packed(last) for last in (D, width, width, width, D)]
        + [jax.ShapeDtypeStruct((length, WIDE), BF)] * seqs,
        compiler_params=params(),
        cost_estimate=pl.CostEstimate(
            flops=2 * seqs * rows * D * (2 * length + 5 * width),
            transcendentals=seqs * rows * width,
            bytes_accessed=seqs * (2 * length * WIDE + rows * (2 * D + 5 * width)) * 2
            + 3 * local_experts * width * D * 2,
        ),
    )(first, *tokens, *cots, grads, gate_weight, up_weight, down_weight, *after)


def mixture_kernel(seqs, local_experts, first_ref, rows_ref, *refs):
    tables, outs, put = refs[:seqs], refs[seqs : 2 * seqs], refs[2 * seqs]
    first = first_ref[0]

    @pl.when(pl.program_id(0) == 0)
    def _():
        for s in range(seqs):
            put[s] = put_matrix(tables[s][...], local_experts, first)

    for s in range(seqs):
        outs[s][...] = dot32(put[s], rows_ref[s].reshape(local_experts * CAP, -1)).astype(BF)


def mixture_call(first, out_rows, cots):
    seqs, local_experts = out_rows.shape[:2]
    length = cots[0].shape[0]
    columns = D // 4
    rows = local_experts * CAP
    return pl.pallas_call(
        functools.partial(mixture_kernel, seqs, local_experts),
        grid_spec=pltpu.PrefetchScalarGridSpec(
            num_scalar_prefetch=1,
            grid=(4,),
            in_specs=[pl.BlockSpec((seqs, local_experts, CAP, columns), lambda c, f: (0, 0, 0, c))]
            + [pl.BlockSpec((length, EXTRA), lambda c, f: (0, D // EXTRA))] * seqs,
            out_specs=[pl.BlockSpec((length, columns), lambda c, f: (0, c))] * seqs,
            scratch_shapes=[pltpu.VMEM((seqs, length, rows), BF)],
        ),
        out_shape=[jax.ShapeDtypeStruct((length, D), BF)] * seqs,
        compiler_params=params(),
        cost_estimate=pl.CostEstimate(
            flops=2 * seqs * rows * length * D,
            transcendentals=0,
            bytes_accessed=seqs * (rows + length) * D * 2,
        ),
    )(first, out_rows, *cots)


def weight_grad_kernel(parts, carried, *refs):
    ins, (gate_ref, up_ref, down_ref), (rows, cots, small) = (
        refs[: 5 * parts],
        refs[5 * parts + carried : 5 * parts + carried + 3],
        refs[5 * parts + carried + 3 :],
    )
    width = gate_ref.shape[2]
    for p in range(parts):
        rows_ref, cot_ref, hidden_ref, grad_gate_ref, grad_up_ref = ins[5 * p : 5 * p + 5]
        count = rows_ref.shape[0] * CAP
        span = pl.ds(p * count, count)
        rows[span] = rows_ref[:, 0].reshape(count, D)
        cots[span] = cot_ref[:, 0].reshape(count, D)
        small[span, :width] = grad_gate_ref[:, 0].reshape(count, width)
        small[span, width : 2 * width] = grad_up_ref[:, 0].reshape(count, width)
        small[span, 2 * width :] = hidden_ref[:, 0].reshape(count, width)
    both = dot32(rows[...].T, small[:, : 2 * width])
    gate_ref[0] = both[:, :width]
    up_ref[0] = both[:, width:]
    down_ref[0] = dot32(small[:, 2 * width :].T, cots[...])


def weight_grads(pieces, parts, first, last, before):
    seqs, local_experts, _, width = pieces[0][2].shape
    if lax.axis_size(EX) != 8:
        rows, cots, hidden, grad_gate, grad_up = (
            jnp.concatenate([piece[i] for piece in pieces], axis=0) for i in range(5)
        )
        return (
            ein("secd,secf->edf", rows, grad_gate),
            ein("secd,secf->edf", rows, grad_up),
            ein("secf,secd->efd", hidden, cots),
        )
    total = len(pieces) * seqs * CAP
    block = lambda wide, part=0: pl.BlockSpec((seqs, 1, CAP, wide), lambda e: (part, e + first, 0, 0))
    out = lambda *shape: pl.BlockSpec((1, *shape), lambda e: (e + first, 0, 0))
    specs = []
    for part in parts:
        specs += [block(D), block(D, part), block(width), block(width), block(width)]
    flat = [array for piece in pieces for array in piece]
    return pl.pallas_call(
        functools.partial(weight_grad_kernel, len(pieces), len(before)),
        grid=(last - first,),
        in_specs=specs + [pl.BlockSpec(memory_space=pl.ANY)] * len(before),
        out_specs=[out(D, width), out(D, width), out(width, D)],
        input_output_aliases={len(flat) + i: i for i in range(len(before))},
        out_shape=[
            jax.ShapeDtypeStruct((local_experts, D, width), F32),
            jax.ShapeDtypeStruct((local_experts, D, width), F32),
            jax.ShapeDtypeStruct((local_experts, width, D), F32),
        ],
        scratch_shapes=[
            pltpu.VMEM((total, D), BF),
            pltpu.VMEM((total, D), BF),
            pltpu.VMEM((total, 3 * width), BF),
        ],
        compiler_params=params(),
        cost_estimate=pl.CostEstimate(
            flops=6 * (last - first) * total * D * width,
            transcendentals=0,
            bytes_accessed=(last - first) * (total * (2 * D + 3 * width) * 2 + 3 * D * width * 4),
        ),
    )(*flat, *before)


def dense_grad_kernel(pairs, tail, owner_ref, *refs):
    lefts, rights = refs[:pairs], refs[pairs : 2 * pairs]
    outs = refs[2 * pairs + tail :]
    rows = D // len(outs)
    for r, out in enumerate(outs):
        span = pl.ds(pl.multiple_of((owner_ref[0] ^ r) * rows, rows), rows)
        column = 0
        for left, right in zip(lefts, rights, strict=True):
            width = right.shape[0]
            turned = left[:, span].T
            out[:rows, column : column + width] = dot_nt(turned, right[...]).astype(BF)
            column = column + width
        if tail:
            out[rows:, :rows] = refs[2 * pairs][:, span]
            out[rows:, rows:] = jnp.zeros((TAIL, column - rows), BF)


def dense_grads(owner, lefts, rights, small=None):
    owners = lax.axis_size(EX)
    rows = D // owners
    width = sum(right.shape[1] for right in rights)
    tail = 0 if small is None else 1
    if owners != 8:
        full = jnp.concatenate(
            [dot32(left[:, :D].T, right) for left, right in zip(lefts, rights, strict=True)], axis=1
        )
        full = full.astype(BF).reshape(owners, rows, width)
        if tail:
            below = jnp.moveaxis(small.reshape(TAIL, owners, rows), 1, 0)
            below = jnp.pad(below, ((0, 0), (0, 0), (0, width - rows)))
            full = jnp.concatenate([full, below], axis=1)
        return [lax.dynamic_index_in_dim(full, owner ^ r, 0, keepdims=False) for r in range(owners)]
    length = lefts[0].shape[0]
    out_rows = rows + TAIL * tail
    vmem = pl.BlockSpec(memory_space=pltpu.VMEM)
    operands = [*lefts, *[right.T for right in rights]] + ([small] if tail else [])
    return pl.pallas_call(
        functools.partial(dense_grad_kernel, len(lefts), tail),
        in_specs=[pl.BlockSpec(memory_space=pltpu.SMEM)] + [vmem] * len(operands),
        out_specs=[vmem] * owners,
        out_shape=[jax.ShapeDtypeStruct((out_rows, width), BF)] * owners,
        compiler_params=pltpu.CompilerParams(vmem_limit_bytes=VMEM_BYTES),
        cost_estimate=pl.CostEstimate(
            flops=2 * length * D * width,
            transcendentals=0,
            bytes_accessed=(len(lefts) * length * D + length * width + D * width) * 2,
        ),
    )(jnp.full((1,), owner, jnp.int32), *operands)


def layer(
    block_input,
    out_grad,
    norm_one,
    query_weight,
    key_weight,
    value_weight,
    query_gain,
    key_gain,
    output_weight,
    norm_two,
    router_weight,
    gate_weight,
    up_weight,
    down_weight,
    segment_ids,
    expert_routes,
    expert_slots,
):
    length = block_input.shape[0]
    local_width = query_weight.shape[1]
    head_count = local_width // HD
    score_scale = HD ** (-0.5)
    groups = lax.axis_size(WE)
    place = lax.axis_index(WE)
    owners = lax.axis_size(EX)
    owner = lax.axis_index(EX)
    local_experts = gate_weight.shape[0]
    first_expert = owner * local_experts
    quarter = length // groups
    col_width = D // groups
    first_row = place * quarter

    chosen = expert_routes[:, :, None] == jnp.arange(EXPERTS)[None, None, :]
    slot_table = jnp.min(jnp.where(chosen, expert_slots[:, :, None], CAP), axis=1).astype(BF)
    slot_turned = lax.dynamic_slice_in_dim(
        jnp.concatenate([slot_table, slot_table], axis=0), first_row, length, 0
    )
    slot_wide = jnp.concatenate([slot_table, slot_turned], axis=1)

    inputs = block_input.astype(F32)
    scale_one = rms_scale(inputs)
    normed_one = (inputs * scale_one * norm_one).astype(BF)
    query_pre = dot32(normed_one, query_weight)
    key_pre = dot32(normed_one, key_weight)
    squares = jnp.stack(
        [jnp.sum(query_pre * query_pre, axis=-1), jnp.sum(key_pre * key_pre, axis=-1)]
    )
    squares = sum_weight_small(squares)
    cotangent = prepare_call(out_grad, slot_wide)
    cotangents_near = gather_start(cotangent)
    value_flat = dot32(normed_one, value_weight).astype(BF)
    query_scale = lax.rsqrt(squares[0] / D + norm_eps)[:, None]
    key_scale = lax.rsqrt(squares[1] / D + norm_eps)[:, None]
    query_gains = query_gain.reshape(-1)
    key_gains = key_gain.reshape(-1)
    head_shape = (length, head_count, HD)
    cosine, sine_table = rope_tables(length, HD)
    query_rot = rotate(
        (query_pre * query_scale * query_gains).reshape(head_shape), cosine, sine_table
    ).astype(BF)
    key_rot = rotate(
        (key_pre * key_scale * key_gains).reshape(head_shape), cosine, sine_table
    ).astype(BF)
    value_heads = value_flat.reshape(head_shape)
    segment_row = segment_ids[0]
    positions = jnp.arange(length)
    allowed = (positions[:, None] >= positions[None, :]) & (
        segment_row[:, None] == segment_row[None, :]
    )
    scores = jnp.where(allowed[None], ein(QK, query_rot, key_rot) * score_scale, -1e30)
    highest = jnp.max(scores, axis=-1, keepdims=True)
    exponent = jnp.exp(scores - highest)
    denominator = jnp.sum(exponent, axis=-1, keepdims=True)
    soft = exponent / denominator
    soft_b = soft.astype(BF)
    attended = ein(QV, soft_b, value_heads).reshape(length, local_width).astype(BF)
    attention_part = dot32(attended, output_weight).astype(BF)
    cotangents = gather_finish(cotangent, cotangents_near)

    input_rows = lax.dynamic_slice_in_dim(block_input, first_row, quarter, 0).astype(F32)
    second = input_rows + scatter_weight(
        lambda step: lax.dynamic_slice_in_dim(
            attention_part, ((place + step) % groups) * quarter, quarter, 0
        ),
    )
    scale_two = rms_scale(second)
    normed_rows = (second * scale_two * norm_two).astype(BF)
    gate_rows = jax.nn.softmax(dot32(normed_rows, router_weight), axis=-1)
    token_rows = jnp.concatenate([normed_rows, *two_parts(gate_rows)], axis=1)
    tokens_own = gather_weight_relative(token_rows)
    tokens = gather_finish(tokens_own, gather_start(tokens_own))

    first_array = jnp.full((1,), first_expert, jnp.int32)
    pairs = [(r, r + 1) for r in range(0, owners, 2)]
    cot_groups = pairs
    if owners == 8:
        pairs = [(0, 1), (2, 3), (6, 7), (4, 5)]
        cot_groups = [(0, 1), (2, 3), (4, 5, 6, 7)]
    cot_rows = {}
    for group in cot_groups:
        both = cotangent_call(first_array, [cotangents[r] for r in group], down_weight)
        for i in range(0, len(group), 2):
            cot_rows[group[i]] = (*both, i // 2)
    after, back, pieces, parts, out_rows = [], {}, [], [], {}
    for pair in pairs:
        rows_grad, grad_hidden, part = cot_rows[pair[0]]
        rows_in, hidden, grad_gate, grad_up, out_rows[pair], *backs = expert_call(
            first_array,
            [tokens[r] for r in pair],
            [cotangents[r] for r in pair],
            grad_hidden,
            part,
            gate_weight,
            up_weight,
            down_weight,
            after,
        )
        after = [hidden]
        pieces.append((rows_in, rows_grad, hidden, grad_gate, grad_up))
        parts.append(part)
        back.update(zip(pair, backs, strict=True))
    expert_grads, done = (), 0
    for limit in (local_experts // 2, local_experts) if owners == 8 else (local_experts,):
        expert_grads = weight_grads(pieces, parts, done, limit, expert_grads)
        done = limit
    gate_result, up_result, down_result = expert_grads
    back_left, back_right = scatter_expert([back[r] for r in range(owners)], D // 2)
    left_rows = scatter_weight(lambda step: back_left[step * quarter : (step + 1) * quarter])
    right_rows = scatter_weight(lambda step: back_right[step * quarter : (step + 1) * quarter])

    mixed_out = {}
    for pair in [(6, 7), (0, 1), (2, 3), (4, 5)] if owners == 8 else pairs:
        outs = mixture_call(first_array, out_rows[pair], [cotangents[r] for r in pair])
        mixed_out.update(zip(pair, outs, strict=True))
    own_rows = lax.dynamic_slice_in_dim(mixed_out[0], first_row, quarter, 0).astype(F32) + second
    mixed_out[0] = lax.dynamic_update_slice_in_dim(mixed_out[0], own_rows.astype(BF), first_row, 0)
    mixture_own = scatter_expert([mixed_out[r] for r in range(owners)])
    block_output = scatter_weight(
        lambda step: lax.dynamic_slice_in_dim(
            mixture_own, ((place + step) % groups) * col_width, col_width, 1
        ),
    )

    grad_probs = right_rows[:, D // 2 : D // 2 + EXPERTS] + right_rows[:, D // 2 + EXPERTS :]
    grad_logits = gate_rows * (grad_probs - jnp.sum(gate_rows * grad_probs, axis=-1, keepdims=True))
    grad_logits_b = grad_logits.astype(BF)
    grad_normed_two = jnp.concatenate([left_rows, right_rows[:, : D // 2]], axis=1)
    grad_normed_two = grad_normed_two + dot32(grad_logits_b, router_weight.T)
    weighted_two = grad_normed_two * norm_two
    norm_two_part = sum_weight_small(jnp.sum(grad_normed_two * second * scale_two, axis=0))
    out_grad_rows = lax.dynamic_slice_in_dim(out_grad, first_row, quarter, 0)
    grad_second = (
        out_grad_rows
        + scale_two * weighted_two
        - second * scale_two**3 * jnp.mean(second * weighted_two, axis=-1, keepdims=True)
    )
    second_rows = jnp.concatenate(
        [grad_second.astype(BF), grad_logits_b, jnp.zeros((quarter, EXTRA - EXPERTS), BF)], axis=1
    )
    second_all = gather_weight(second_rows)
    grad_second_b = second_all[:, :D]

    grad_mixed = dot_nt(grad_second_b, output_weight).astype(BF).reshape(head_shape)
    grad_soft = ein(QK, grad_mixed, value_heads)
    inner = jnp.sum(soft * grad_soft, axis=-1, keepdims=True)
    grad_scores = (soft * (grad_soft - inner)).astype(BF)
    grad_query_rot = ein(QV, grad_scores, key_rot) * score_scale
    grad_key_rot = ein(KV, grad_scores, query_rot) * score_scale
    grad_values_b = ein(KV, soft_b, grad_mixed).reshape(length, local_width).astype(BF)
    grad_query_norm = rotate_back(grad_query_rot, cosine, sine_table).reshape(length, local_width)
    grad_key_norm = rotate_back(grad_key_rot, cosine, sine_table).reshape(length, local_width)
    weighted_query = grad_query_norm * query_gains
    weighted_key = grad_key_norm * key_gains
    query_gain_part = jnp.sum(grad_query_norm * query_pre * query_scale, axis=0)
    key_gain_part = jnp.sum(grad_key_norm * key_pre * key_scale, axis=0)
    cross = jnp.stack(
        [jnp.sum(query_pre * weighted_query, axis=-1), jnp.sum(key_pre * weighted_key, axis=-1)]
    )
    cross = sum_weight_small(cross)
    sums_a = dense_grads(owner, [normed_one, second_all], [grad_values_b, attended])
    reduced_a = scatter_expert(sums_a)
    grad_query_pre = (
        query_scale * weighted_query - query_pre * query_scale**3 * (cross[0] / D)[:, None]
    ).astype(BF)
    grad_key_pre = (
        key_scale * weighted_key - key_pre * key_scale**3 * (cross[1] / D)[:, None]
    ).astype(BF)
    grad_normed_local = (
        dot_nt(grad_query_pre, query_weight)
        + dot_nt(grad_key_pre, key_weight)
        + dot_nt(grad_values_b, value_weight)
    )
    inputs_again = lax.optimization_barrier(block_input).astype(F32)
    norm_one_part = jnp.sum(grad_normed_local * inputs_again * scale_one, axis=0)
    grad_normed_one = scatter_weight(
        lambda step: lax.dynamic_slice_in_dim(
            grad_normed_local, ((place + step) % groups) * quarter, quarter, 0
        ),
    )
    scale_rows = lax.dynamic_slice_in_dim(scale_one, first_row, quarter, 0)
    weighted_one = grad_normed_one * norm_one
    input_result = (
        grad_second
        + scale_rows * weighted_one
        - input_rows * scale_rows**3 * jnp.mean(input_rows * weighted_one, axis=-1, keepdims=True)
    )

    router_cols = EXPERTS // groups
    logits_mine = lax.dynamic_slice_in_dim(second_all, D + place * router_cols, router_cols, 1)
    tokens_turned = lax.dynamic_slice_in_dim(
        jnp.concatenate([logits_mine, logits_mine], axis=0), first_row, length, 0
    )
    router_part = lax.dot_general(
        tokens_turned, tokens_own[:, :D], (((0,), (0,)), ((), ())), preferred_element_type=F32
    )
    rows = D // owners
    gain_width = HD // owners
    gains = jnp.concatenate([query_gain_part, key_gain_part]).reshape(2 * head_count, owners, gain_width)
    gains = jnp.pad(gains, ((0, 0), (0, 0), (0, rows - gain_width))).reshape(2 * head_count, D)
    small = jnp.concatenate([router_part, norm_one_part[None], norm_two_part[None], gains], axis=0)
    small = jnp.pad(small, ((0, TAIL - small.shape[0]), (0, 0))).astype(BF)
    sums_b = dense_grads(owner, [normed_one, normed_one], [grad_query_pre, grad_key_pre], small)
    reduced_b = scatter_expert(sums_b)
    tail = reduced_b[rows:, :rows]
    norm_one_result = sum_weight_small(tail[router_cols])
    gain_result = tail[router_cols + 2 : router_cols + 2 + 2 * head_count, :gain_width]
    width = local_width
    return (
        block_output,
        input_result,
        norm_one_result,
        reduced_b[:rows, :width],
        reduced_b[:rows, width:],
        reduced_a[:, :width],
        gain_result[:head_count],
        gain_result[head_count:],
        reduced_a[:, width:].T,
        tail[router_cols + 1],
        tail[:router_cols].T,
        gate_result,
        up_result,
        down_result,
    )


def solution(mesh):
    rows = P(EX, None)
    columns = P(None, WE)
    heads = P(WE, None)
    mixed = P(EX, None, WE)
    down = P(EX, WE, None)
    in_specs = (
        (rows, rows, P(), columns, columns, columns, heads, heads, heads)
        + (P(), P(), mixed, mixed, down, rows, rows, rows)
    )
    square = P(EX, WE)
    turned = P(WE, EX)
    out_specs = (
        (square, P((EX, WE), None), P(EX), square, square, square)
        + (turned, turned, turned, P(EX), square, mixed, mixed, down)
    )
    return jax.shard_map(layer, mesh=mesh, in_specs=in_specs, out_specs=out_specs, check_vma=False)
```

```python
import functools

import jax
import jax.numpy as jnp
from jax import lax
from jax.experimental import pallas as pl
from jax.experimental.pallas import tpu as pltpu
from jax.sharding import PartitionSpec as P

D = 2048
HD = 128
EXPERTS = 64
CAP = 96
EXTRA = 128
WIDE = D + EXTRA
TAIL = 32
BF = jnp.bfloat16
F32 = jnp.float32
NT = (((1,), (1,)), ((), ()))
VMEM_BYTES = 67_000_000
EX = "expert"
WE = "weight"
GRID1 = ("arbitrary",)
QK = "qhd,khd->hqk"
QV = "hqk,khd->qhd"
KV = "hqk,qhd->khd"

norm_eps = 1e-05
rope_base = 10000.0


def rms_scale(values):
    return lax.rsqrt(jnp.mean(values * values, axis=-1, keepdims=True) + norm_eps)


def rope_tables(length, head_width):
    exponent = jnp.arange(head_width // 2).astype(F32) * 2.0 / head_width
    inverse = rope_base ** (-exponent)
    angles = jnp.arange(length).astype(F32)[:, None] * inverse[None, :]
    angles = jnp.concatenate([angles, angles], axis=-1)[:, None, :]
    return (jnp.cos(angles), jnp.sin(angles))


def rotate(values, cosine, sine_table):
    half_width = values.shape[-1] // 2
    turned = jnp.concatenate([-values[..., half_width:], values[..., :half_width]], axis=-1)
    return values * cosine + turned * sine_table


def rotate_back(values, cosine, sine_table):
    half_width = values.shape[-1] // 2
    shifted = values * sine_table
    turned = jnp.concatenate([shifted[..., half_width:], -shifted[..., :half_width]], axis=-1)
    return values * cosine + turned


def dot32(left, right):
    return jnp.dot(left, right, preferred_element_type=F32)


def ein(spec, left, right):
    return jnp.einsum(spec, left, right, preferred_element_type=F32)


def dot_nt(left, right):
    return lax.dot_general(left, right, NT, preferred_element_type=F32)


def swap(values, distance):
    count = lax.axis_size(EX)
    return lax.ppermute(values, EX, [(i, i ^ distance) for i in range(count)])


def swap_weight(values, distance):
    count = lax.axis_size(WE)
    return lax.ppermute(values, WE, [(i, i ^ distance) for i in range(count)])


def shift_weight(values, distance):
    count = lax.axis_size(WE)
    return lax.ppermute(values, WE, [(i, (i + distance) % count) for i in range(count)])


def gather_start(block):
    if lax.axis_size(EX) != 8:
        return ()
    return (swap(block, 2), swap(block, 4))


def gather_finish(block, near):
    count = lax.axis_size(EX)
    if count != 8:
        return [block] + [swap(block, r) for r in range(1, count)]
    half = block.shape[0] // 2
    from_x, from_y = near
    diagonal = jnp.concatenate([swap(from_y[:half], 2), swap(from_x[half:], 4)], axis=0)
    blocks = []
    for own in (block, from_x, from_y, diagonal):
        blocks += [own, swap(own, 1)]
    return blocks


def scatter_expert(parts, cut=0):
    count = lax.axis_size(EX)
    if count != 8:
        total = parts[0].astype(F32)
        for r in range(1, count):
            total = total + swap(parts[r], r).astype(F32)
        return (total[:, :cut], total[:, cut:]) if cut else total
    sums = {r: parts[r].astype(F32) + swap(parts[r ^ 1], 1).astype(F32) for r in (6, 2, 4, 0)}
    half = sums[6].shape[0] // 2
    far = sums[6].astype(BF)
    over_x = swap(far[:half], 2).astype(F32)
    over_y = swap(far[half:], 4).astype(F32)
    to_y = jnp.concatenate([sums[4][:half] + over_x, sums[4][half:]], axis=0).astype(BF)
    to_x = jnp.concatenate([sums[2][:half], sums[2][half:] + over_y], axis=0).astype(BF)
    if cut == 0:
        return sums[0] + swap(to_x, 2).astype(F32) + swap(to_y, 4).astype(F32)
    return tuple(
        sums[0][:, span]
        + swap(to_x[:, span], 2).astype(F32)
        + swap(to_y[:, span], 4).astype(F32)
        for span in (slice(0, cut), slice(cut, None))
    )


def sum_weight_small(values):
    distance = 1
    while distance < lax.axis_size(WE):
        values = values + swap_weight(values, distance)
        distance = distance * 2
    return values


def scatter_weight(pick):
    own = pick(0).astype(F32)
    others = [shift_weight(pick(step).astype(BF), step) for step in range(1, lax.axis_size(WE))]
    return functools.reduce(lambda total, other: total + other.astype(F32), others, own)


def gather_weight_relative(block):
    blocks = [block]
    for step in range(1, lax.axis_size(WE)):
        blocks.append(shift_weight(block, -step))
    return jnp.concatenate(blocks, axis=0)


def gather_weight(block):
    count = lax.axis_size(WE)
    place = lax.axis_index(WE)
    rows = block.shape[0]
    blocks = [block] + [shift_weight(block, step) for step in range(1, count)]
    whole = jnp.zeros((count * rows,) + block.shape[1:], block.dtype)
    for step, one in enumerate(blocks):
        whole = lax.dynamic_update_slice_in_dim(whole, one, ((place - step) % count) * rows, 0)
    return whole


def two_parts(values):
    high = values.astype(BF)
    low = (values - high.astype(F32)).astype(BF)
    return high, low


def row_places(shape, axis, first_lane):
    row = lax.broadcasted_iota(jnp.int32, shape, axis)
    expert = (row * 683) >> 16
    return first_lane + expert, row - expert * CAP


def pick_matrix(table, local_experts, first_lane):
    rows = local_experts * CAP
    expert, _ = row_places((rows, EXTRA), 0, first_lane)
    lane = lax.broadcasted_iota(jnp.int32, (rows, EXTRA), 1)
    wanted = dot_nt((lane == expert).astype(BF), table)
    _, slot = row_places(wanted.shape, 0, first_lane)
    return (wanted == slot.astype(F32)).astype(BF)


def put_matrix(table, local_experts, first_lane):
    rows = local_experts * CAP
    expert, _ = row_places((EXTRA, rows), 1, first_lane)
    lane = lax.broadcasted_iota(jnp.int32, (EXTRA, rows), 0)
    wanted = dot32(table, (lane == expert).astype(BF))
    _, slot = row_places(wanted.shape, 1, first_lane)
    return (wanted == slot.astype(F32)).astype(BF)


def params():
    return pltpu.CompilerParams(dimension_semantics=GRID1, vmem_limit_bytes=VMEM_BYTES)


def prepare_kernel(grad_ref, slot_ref, out_ref):
    out_ref[:, :D] = grad_ref[...].astype(BF)
    out_ref[:, D:] = slot_ref[...]


def prepare_call(out_grad, slot_wide):
    length = out_grad.shape[0]
    rows = length // 4
    return pl.pallas_call(
        prepare_kernel,
        grid=(4,),
        in_specs=[pl.BlockSpec((rows, D), lambda i: (i, 0)), pl.BlockSpec((rows, EXTRA), lambda i: (i, 0))],
        out_specs=pl.BlockSpec((rows, WIDE), lambda i: (i, 0)),
        out_shape=jax.ShapeDtypeStruct((length, WIDE), BF),
        cost_estimate=pl.CostEstimate(
            flops=length * D, transcendentals=0, bytes_accessed=length * WIDE * 6
        ),
    )(out_grad, slot_wide)


def cotangent_kernel(seqs, local_experts, first_ref, *refs):
    cots = refs[:seqs]
    down_ref = refs[seqs]
    rows_ref, hidden_ref, held = refs[seqs + 1 :]
    e = pl.program_id(0)
    first = first_ref[0]

    @pl.when(e == 0)
    def _():
        for s in range(seqs):
            pick = pick_matrix(cots[s][:, D:], local_experts, first)
            held[s] = dot32(pick, cots[s][:, :D]).astype(BF)

    rows = held[:, pl.ds(pl.multiple_of(e * CAP, CAP), CAP), :]
    rows_ref[:, 0] = rows
    hidden_ref[:, 0] = dot_nt(rows.reshape(seqs * CAP, D), down_ref[0]).reshape(seqs, CAP, -1)


def cotangent_call(first, cots, down_weight):
    seqs = len(cots)
    local_experts, width, _ = down_weight.shape
    length = cots[0].shape[0]
    whole = pl.BlockSpec((length, WIDE), lambda e, f: (0, 0), pipeline_mode=pl.Buffered(1))
    return pl.pallas_call(
        functools.partial(cotangent_kernel, seqs, local_experts),
        grid_spec=pltpu.PrefetchScalarGridSpec(
            num_scalar_prefetch=1,
            grid=(local_experts,),
            in_specs=[whole] * seqs + [pl.BlockSpec((1, width, D), lambda e, f: (e, 0, 0))],
            out_specs=[
                pl.BlockSpec((seqs, 1, CAP, D), lambda e, f: (0, e, 0, 0)),
                pl.BlockSpec((seqs, 1, CAP, width), lambda e, f: (0, e, 0, 0)),
            ],
            scratch_shapes=[pltpu.VMEM((seqs, local_experts * CAP, D), BF)],
        ),
        out_shape=[
            jax.ShapeDtypeStruct((seqs, local_experts, CAP, D), BF),
            jax.ShapeDtypeStruct((seqs, local_experts, CAP, width), F32),
        ],
        compiler_params=params(),
        cost_estimate=pl.CostEstimate(
            flops=2 * seqs * local_experts * CAP * D * (length + width),
            transcendentals=0,
            bytes_accessed=seqs * (length * WIDE + local_experts * CAP * (D + 2 * width)) * 2
            + local_experts * width * D * 2,
        ),
    )(first, *cots, down_weight)


def expert_kernel(seqs, local_experts, extra, first_ref, *refs):
    tokens = refs[:seqs]
    tables = refs[seqs : 2 * seqs]
    grad_ref, gate_ref, up_ref, down_ref = refs[2 * seqs : 2 * seqs + 4]
    rest = refs[2 * seqs + 4 + extra :]
    rows_ref, hidden_ref, grad_gate_ref, grad_up_ref, out_ref = rest[:5]
    backs = rest[5 : 5 + seqs]
    held = rest[5 + seqs]
    e = pl.program_id(0)
    first = first_ref[0]
    count = seqs * CAP

    @pl.when(e == 0)
    def _():
        for s in range(seqs):
            pick = pick_matrix(tables[s][...], local_experts, first + EXPERTS)
            held[s] = dot32(pick, tokens[s][...]).astype(BF)

    span = pl.ds(pl.multiple_of(e * CAP, CAP), CAP)
    both = held[:, span, :].reshape(count, WIDE)
    rows = both[:, :D]
    rows_ref[:, 0] = rows.reshape(seqs, CAP, D)
    lane = lax.broadcasted_iota(jnp.int32, (count, EXTRA), 1)
    own_high = lane == first + e
    own_low = lane == first + e + EXPERTS
    gates = jnp.sum(
        jnp.where(own_high | own_low, both[:, D:].astype(F32), 0.0), axis=1, keepdims=True
    )
    gate_pre = dot32(rows, gate_ref[0])
    up_pre = dot32(rows, up_ref[0])
    grad_hidden = grad_ref[:, 0].reshape(count, -1)
    sigmoid_gate = jax.nn.sigmoid(gate_pre)
    silu_gate = gate_pre * sigmoid_gate
    hidden = silu_gate * up_pre
    gated = (gates * hidden).astype(BF)
    gate_grads = jnp.sum(hidden * grad_hidden, axis=1, keepdims=True)
    grad_hidden = gates * grad_hidden
    grad_gate = (
        grad_hidden * up_pre * sigmoid_gate * (1.0 + gate_pre * (1.0 - sigmoid_gate))
    ).astype(BF)
    grad_up = (grad_hidden * silu_gate).astype(BF)
    hidden_ref[:, 0] = gated.reshape(seqs, CAP, -1)
    grad_gate_ref[:, 0] = grad_gate.reshape(seqs, CAP, -1)
    grad_up_ref[:, 0] = grad_up.reshape(seqs, CAP, -1)
    out_ref[:, 0] = dot32(gated, down_ref[0]).astype(BF).reshape(seqs, CAP, D)
    back = dot_nt(grad_gate, gate_ref[0]) + dot_nt(grad_up, up_ref[0])
    held[:, span, :D] = back.astype(BF).reshape(seqs, CAP, D)
    high = gate_grads.astype(BF).astype(F32)
    spread = jnp.where(own_high, high, jnp.where(own_low, gate_grads - high, 0.0))
    held[:, span, D:] = spread.astype(BF).reshape(seqs, CAP, EXTRA)

    @pl.when(e == local_experts - 1)
    def _():
        for s in range(seqs):
            put = put_matrix(tables[s][...], local_experts, first + EXPERTS)
            backs[s][...] = dot32(put, held[s]).astype(BF)


def expert_call(first, tokens, cots, grads, part, gate_weight, up_weight, down_weight, after):
    seqs = len(tokens)
    local_experts, width, _ = down_weight.shape
    length = tokens[0].shape[0]
    rows = local_experts * CAP
    once = pl.Buffered(1)
    per_expert = lambda last, part=0: pl.BlockSpec((seqs, 1, CAP, last), lambda e, f: (part, e, 0, 0))
    packed = lambda last: jax.ShapeDtypeStruct((seqs, local_experts, CAP, last), BF)
    return pl.pallas_call(
        functools.partial(expert_kernel, seqs, local_experts, len(after)),
        grid_spec=pltpu.PrefetchScalarGridSpec(
            num_scalar_prefetch=1,
            grid=(local_experts,),
            in_specs=[pl.BlockSpec((length, WIDE), lambda e, f: (0, 0), pipeline_mode=once)] * seqs
            + [pl.BlockSpec((length, EXTRA), lambda e, f: (0, D // EXTRA), pipeline_mode=once)] * seqs
            + [
                per_expert(width, part),
                pl.BlockSpec((1, D, width), lambda e, f: (e, 0, 0)),
                pl.BlockSpec((1, D, width), lambda e, f: (e, 0, 0)),
                pl.BlockSpec((1, width, D), lambda e, f: (e, 0, 0)),
            ]
            + [pl.BlockSpec(memory_space=pl.ANY)] * len(after),
            out_specs=[per_expert(last) for last in (D, width, width, width, D)]
            + [pl.BlockSpec((length, WIDE), lambda e, f: (0, 0), pipeline_mode=once)] * seqs,
            scratch_shapes=[pltpu.VMEM((seqs, rows, WIDE), BF)],
        ),
        out_shape=[packed(last) for last in (D, width, width, width, D)]
        + [jax.ShapeDtypeStruct((length, WIDE), BF)] * seqs,
        compiler_params=params(),
        cost_estimate=pl.CostEstimate(
            flops=2 * seqs * rows * D * (2 * length + 5 * width),
            transcendentals=seqs * rows * width,
            bytes_accessed=seqs * (2 * length * WIDE + rows * (2 * D + 5 * width)) * 2
            + 3 * local_experts * width * D * 2,
        ),
    )(first, *tokens, *cots, grads, gate_weight, up_weight, down_weight, *after)


def mixture_kernel(seqs, local_experts, first_ref, rows_ref, *refs):
    tables, outs, put = refs[:seqs], refs[seqs : 2 * seqs], refs[2 * seqs]
    first = first_ref[0]

    @pl.when(pl.program_id(0) == 0)
    def _():
        for s in range(seqs):
            put[s] = put_matrix(tables[s][...], local_experts, first)

    for s in range(seqs):
        outs[s][...] = dot32(put[s], rows_ref[s].reshape(local_experts * CAP, -1)).astype(BF)


def mixture_call(first, out_rows, cots):
    seqs, local_experts = out_rows.shape[:2]
    length = cots[0].shape[0]
    columns = D // 4
    rows = local_experts * CAP
    return pl.pallas_call(
        functools.partial(mixture_kernel, seqs, local_experts),
        grid_spec=pltpu.PrefetchScalarGridSpec(
            num_scalar_prefetch=1,
            grid=(4,),
            in_specs=[pl.BlockSpec((seqs, local_experts, CAP, columns), lambda c, f: (0, 0, 0, c))]
            + [pl.BlockSpec((length, EXTRA), lambda c, f: (0, D // EXTRA))] * seqs,
            out_specs=[pl.BlockSpec((length, columns), lambda c, f: (0, c))] * seqs,
            scratch_shapes=[pltpu.VMEM((seqs, length, rows), BF)],
        ),
        out_shape=[jax.ShapeDtypeStruct((length, D), BF)] * seqs,
        compiler_params=params(),
        cost_estimate=pl.CostEstimate(
            flops=2 * seqs * rows * length * D,
            transcendentals=0,
            bytes_accessed=seqs * (rows + length) * D * 2,
        ),
    )(first, out_rows, *cots)


def weight_grad_kernel(parts, carried, *refs):
    ins, (gate_ref, up_ref, down_ref), (rows, cots, small) = (
        refs[: 5 * parts],
        refs[5 * parts + carried : 5 * parts + carried + 3],
        refs[5 * parts + carried + 3 :],
    )
    width = gate_ref.shape[2]
    for p in range(parts):
        rows_ref, cot_ref, hidden_ref, grad_gate_ref, grad_up_ref = ins[5 * p : 5 * p + 5]
        count = rows_ref.shape[0] * CAP
        span = pl.ds(p * count, count)
        rows[span] = rows_ref[:, 0].reshape(count, D)
        cots[span] = cot_ref[:, 0].reshape(count, D)
        small[span, :width] = grad_gate_ref[:, 0].reshape(count, width)
        small[span, width : 2 * width] = grad_up_ref[:, 0].reshape(count, width)
        small[span, 2 * width :] = hidden_ref[:, 0].reshape(count, width)
    both = dot32(rows[...].T, small[:, : 2 * width])
    gate_ref[0] = both[:, :width]
    up_ref[0] = both[:, width:]
    down_ref[0] = dot32(small[:, 2 * width :].T, cots[...])


def weight_grads(pieces, parts, first, last, before):
    seqs, local_experts, _, width = pieces[0][2].shape
    if lax.axis_size(EX) != 8:
        rows, cots, hidden, grad_gate, grad_up = (
            jnp.concatenate([piece[i] for piece in pieces], axis=0) for i in range(5)
        )
        return (
            ein("secd,secf->edf", rows, grad_gate),
            ein("secd,secf->edf", rows, grad_up),
            ein("secf,secd->efd", hidden, cots),
        )
    total = len(pieces) * seqs * CAP
    block = lambda wide, part=0: pl.BlockSpec((seqs, 1, CAP, wide), lambda e: (part, e + first, 0, 0))
    out = lambda *shape: pl.BlockSpec((1, *shape), lambda e: (e + first, 0, 0))
    specs = []
    for part in parts:
        specs += [block(D), block(D, part), block(width), block(width), block(width)]
    flat = [array for piece in pieces for array in piece]
    return pl.pallas_call(
        functools.partial(weight_grad_kernel, len(pieces), len(before)),
        grid=(last - first,),
        in_specs=specs + [pl.BlockSpec(memory_space=pl.ANY)] * len(before),
        out_specs=[out(D, width), out(D, width), out(width, D)],
        input_output_aliases={len(flat) + i: i for i in range(len(before))},
        out_shape=[
            jax.ShapeDtypeStruct((local_experts, D, width), F32),
            jax.ShapeDtypeStruct((local_experts, D, width), F32),
            jax.ShapeDtypeStruct((local_experts, width, D), F32),
        ],
        scratch_shapes=[
            pltpu.VMEM((total, D), BF),
            pltpu.VMEM((total, D), BF),
            pltpu.VMEM((total, 3 * width), BF),
        ],
        compiler_params=params(),
        cost_estimate=pl.CostEstimate(
            flops=6 * (last - first) * total * D * width,
            transcendentals=0,
            bytes_accessed=(last - first) * (total * (2 * D + 3 * width) * 2 + 3 * D * width * 4),
        ),
    )(*flat, *before)


def dense_grad_kernel(counts, owner_ref, *refs):
    lefts = refs[: len(counts)]
    rights = refs[len(counts) : len(counts) + sum(counts)]
    small, *outs = refs[len(counts) + sum(counts) :]
    rows = D // len(outs)
    for r, out in enumerate(outs):
        span = pl.ds(pl.multiple_of((owner_ref[0] ^ r) * rows, rows), rows)
        column, at = 0, 0
        for left, count in zip(lefts, counts, strict=True):
            turned = left[:, span].T
            for right in rights[at : at + count]:
                width = right.shape[0]
                out[:rows, column : column + width] = dot_nt(turned, right[...]).astype(BF)
                column = column + width
            at = at + count
        out[rows:, :rows] = small[:, span]
        out[rows:, rows:] = jnp.zeros((TAIL, column - rows), BF)


def dense_grads(owner, groups, small):
    owners = lax.axis_size(EX)
    rows = D // owners
    lefts = [left for left, _ in groups]
    rights = [right for _, some in groups for right in some]
    width = sum(right.shape[1] for right in rights)
    if owners != 8:
        full = [dot32(left[:, :D].T, right) for left, some in groups for right in some]
        full = jnp.concatenate(full, axis=1).astype(BF).reshape(owners, rows, width)
        below = jnp.moveaxis(small.reshape(TAIL, owners, rows), 1, 0)
        below = jnp.pad(below, ((0, 0), (0, 0), (0, width - rows)))
        full = jnp.concatenate([full, below], axis=1)
        return [lax.dynamic_index_in_dim(full, owner ^ r, 0, keepdims=False) for r in range(owners)]
    length = lefts[0].shape[0]
    vmem = pl.BlockSpec(memory_space=pltpu.VMEM)
    operands = [*lefts, *[right.T for right in rights], small]
    return pl.pallas_call(
        functools.partial(dense_grad_kernel, [len(some) for _, some in groups]),
        in_specs=[pl.BlockSpec(memory_space=pltpu.SMEM)] + [vmem] * len(operands),
        out_specs=[vmem] * owners,
        out_shape=[jax.ShapeDtypeStruct((rows + TAIL, width), BF)] * owners,
        compiler_params=pltpu.CompilerParams(vmem_limit_bytes=VMEM_BYTES),
        cost_estimate=pl.CostEstimate(
            flops=2 * length * D * width,
            transcendentals=0,
            bytes_accessed=(len(lefts) * length * D + length * width + D * width) * 2,
        ),
    )(jnp.full((1,), owner, jnp.int32), *operands)


def layer(
    block_input,
    out_grad,
    norm_one,
    query_weight,
    key_weight,
    value_weight,
    query_gain,
    key_gain,
    output_weight,
    norm_two,
    router_weight,
    gate_weight,
    up_weight,
    down_weight,
    segment_ids,
    expert_routes,
    expert_slots,
):
    length = block_input.shape[0]
    local_width = query_weight.shape[1]
    head_count = local_width // HD
    score_scale = HD ** (-0.5)
    groups = lax.axis_size(WE)
    place = lax.axis_index(WE)
    owners = lax.axis_size(EX)
    owner = lax.axis_index(EX)
    local_experts = gate_weight.shape[0]
    first_expert = owner * local_experts
    quarter = length // groups
    col_width = D // groups
    first_row = place * quarter

    chosen = expert_routes[:, :, None] == jnp.arange(EXPERTS)[None, None, :]
    slot_table = jnp.min(jnp.where(chosen, expert_slots[:, :, None], CAP), axis=1).astype(BF)
    slot_turned = lax.dynamic_slice_in_dim(
        jnp.concatenate([slot_table, slot_table], axis=0), first_row, length, 0
    )
    slot_wide = jnp.concatenate([slot_table, slot_turned], axis=1)

    inputs = block_input.astype(F32)
    scale_one = rms_scale(inputs)
    normed_one = (inputs * scale_one * norm_one).astype(BF)
    query_pre = dot32(normed_one, query_weight)
    key_pre = dot32(normed_one, key_weight)
    squares = jnp.stack(
        [jnp.sum(query_pre * query_pre, axis=-1), jnp.sum(key_pre * key_pre, axis=-1)]
    )
    squares = sum_weight_small(squares)
    cotangent = prepare_call(out_grad, slot_wide)
    cotangents_near = gather_start(cotangent)
    value_flat = dot32(normed_one, value_weight).astype(BF)
    query_scale = lax.rsqrt(squares[0] / D + norm_eps)[:, None]
    key_scale = lax.rsqrt(squares[1] / D + norm_eps)[:, None]
    query_gains = query_gain.reshape(-1)
    key_gains = key_gain.reshape(-1)
    head_shape = (length, head_count, HD)
    cosine, sine_table = rope_tables(length, HD)
    query_rot = rotate(
        (query_pre * query_scale * query_gains).reshape(head_shape), cosine, sine_table
    ).astype(BF)
    key_rot = rotate(
        (key_pre * key_scale * key_gains).reshape(head_shape), cosine, sine_table
    ).astype(BF)
    value_heads = value_flat.reshape(head_shape)
    segment_row = segment_ids[0]
    positions = jnp.arange(length)
    allowed = (positions[:, None] >= positions[None, :]) & (
        segment_row[:, None] == segment_row[None, :]
    )
    scores = jnp.where(allowed[None], ein(QK, query_rot, key_rot) * score_scale, -1e30)
    highest = jnp.max(scores, axis=-1, keepdims=True)
    exponent = jnp.exp(scores - highest)
    denominator = jnp.sum(exponent, axis=-1, keepdims=True)
    soft = exponent / denominator
    soft_b = soft.astype(BF)
    attended = ein(QV, soft_b, value_heads).reshape(length, local_width).astype(BF)
    attention_part = dot32(attended, output_weight).astype(BF)
    cotangents = gather_finish(cotangent, cotangents_near)

    input_rows = lax.dynamic_slice_in_dim(block_input, first_row, quarter, 0).astype(F32)
    second = input_rows + scatter_weight(
        lambda step: lax.dynamic_slice_in_dim(
            attention_part, ((place + step) % groups) * quarter, quarter, 0
        ),
    )
    scale_two = rms_scale(second)
    normed_rows = (second * scale_two * norm_two).astype(BF)
    gate_rows = jax.nn.softmax(dot32(normed_rows, router_weight), axis=-1)
    token_rows = jnp.concatenate([normed_rows, *two_parts(gate_rows)], axis=1)
    tokens_own = gather_weight_relative(token_rows)
    tokens = gather_finish(tokens_own, gather_start(tokens_own))

    first_array = jnp.full((1,), first_expert, jnp.int32)
    pairs = [(r, r + 1) for r in range(0, owners, 2)]
    cot_groups = pairs
    if owners == 8:
        pairs = [(0, 1), (2, 3), (6, 7), (4, 5)]
        cot_groups = [(0, 1), (2, 3), (4, 5, 6, 7)]
    cot_rows = {}
    for group in cot_groups:
        both = cotangent_call(first_array, [cotangents[r] for r in group], down_weight)
        for i in range(0, len(group), 2):
            cot_rows[group[i]] = (*both, i // 2)
    after, back, pieces, parts, out_rows = [], {}, [], [], {}
    for pair in pairs:
        rows_grad, grad_hidden, part = cot_rows[pair[0]]
        rows_in, hidden, grad_gate, grad_up, out_rows[pair], *backs = expert_call(
            first_array,
            [tokens[r] for r in pair],
            [cotangents[r] for r in pair],
            grad_hidden,
            part,
            gate_weight,
            up_weight,
            down_weight,
            after,
        )
        after = [hidden]
        pieces.append((rows_in, rows_grad, hidden, grad_gate, grad_up))
        parts.append(part)
        back.update(zip(pair, backs, strict=True))
    expert_grads, done = (), 0
    for limit in (local_experts // 2, local_experts * 3 // 4, local_experts) if owners == 8 else (local_experts,):
        expert_grads = weight_grads(pieces, parts, done, limit, expert_grads)
        done = limit
    gate_result, up_result, down_result = expert_grads
    back_left, back_right = scatter_expert([back[r] for r in range(owners)], D // 2)
    left_rows = scatter_weight(lambda step: back_left[step * quarter : (step + 1) * quarter])
    right_rows = scatter_weight(lambda step: back_right[step * quarter : (step + 1) * quarter])

    mixed_out = {}
    for pair in [(6, 7), (0, 1), (2, 3), (4, 5)] if owners == 8 else pairs:
        outs = mixture_call(first_array, out_rows[pair], [cotangents[r] for r in pair])
        mixed_out.update(zip(pair, outs, strict=True))
    own_rows = lax.dynamic_slice_in_dim(mixed_out[0], first_row, quarter, 0).astype(F32) + second
    mixed_out[0] = lax.dynamic_update_slice_in_dim(mixed_out[0], own_rows.astype(BF), first_row, 0)
    mixture_own = scatter_expert([mixed_out[r] for r in range(owners)])
    block_output = scatter_weight(
        lambda step: lax.dynamic_slice_in_dim(
            mixture_own, ((place + step) % groups) * col_width, col_width, 1
        ),
    )

    grad_probs = right_rows[:, D // 2 : D // 2 + EXPERTS] + right_rows[:, D // 2 + EXPERTS :]
    grad_logits = gate_rows * (grad_probs - jnp.sum(gate_rows * grad_probs, axis=-1, keepdims=True))
    grad_logits_b = grad_logits.astype(BF)
    grad_normed_two = jnp.concatenate([left_rows, right_rows[:, : D // 2]], axis=1)
    grad_normed_two = grad_normed_two + dot32(grad_logits_b, router_weight.T)
    weighted_two = grad_normed_two * norm_two
    norm_two_part = sum_weight_small(jnp.sum(grad_normed_two * second * scale_two, axis=0))
    out_grad_rows = lax.dynamic_slice_in_dim(out_grad, first_row, quarter, 0)
    grad_second = (
        out_grad_rows
        + scale_two * weighted_two
        - second * scale_two**3 * jnp.mean(second * weighted_two, axis=-1, keepdims=True)
    )
    second_rows = jnp.concatenate(
        [grad_second.astype(BF), grad_logits_b, jnp.zeros((quarter, EXTRA - EXPERTS), BF)], axis=1
    )
    second_all = gather_weight(second_rows)
    grad_second_b = second_all[:, :D]

    grad_mixed = dot_nt(grad_second_b, output_weight).astype(BF).reshape(head_shape)
    grad_soft = ein(QK, grad_mixed, value_heads)
    inner = jnp.sum(soft * grad_soft, axis=-1, keepdims=True)
    grad_scores = (soft * (grad_soft - inner)).astype(BF)
    grad_query_rot = ein(QV, grad_scores, key_rot) * score_scale
    grad_key_rot = ein(KV, grad_scores, query_rot) * score_scale
    grad_values_b = ein(KV, soft_b, grad_mixed).reshape(length, local_width).astype(BF)
    grad_query_norm = rotate_back(grad_query_rot, cosine, sine_table).reshape(length, local_width)
    grad_key_norm = rotate_back(grad_key_rot, cosine, sine_table).reshape(length, local_width)
    weighted_query = grad_query_norm * query_gains
    weighted_key = grad_key_norm * key_gains
    query_gain_part = jnp.sum(grad_query_norm * query_pre * query_scale, axis=0)
    key_gain_part = jnp.sum(grad_key_norm * key_pre * key_scale, axis=0)
    cross = jnp.stack(
        [jnp.sum(query_pre * weighted_query, axis=-1), jnp.sum(key_pre * weighted_key, axis=-1)]
    )
    cross = sum_weight_small(cross)
    grad_query_pre = (
        query_scale * weighted_query - query_pre * query_scale**3 * (cross[0] / D)[:, None]
    ).astype(BF)
    grad_key_pre = (
        key_scale * weighted_key - key_pre * key_scale**3 * (cross[1] / D)[:, None]
    ).astype(BF)
    grad_normed_local = (
        dot_nt(grad_query_pre, query_weight)
        + dot_nt(grad_key_pre, key_weight)
        + dot_nt(grad_values_b, value_weight)
    )
    inputs_again = lax.optimization_barrier(block_input).astype(F32)
    norm_one_part = jnp.sum(grad_normed_local * inputs_again * scale_one, axis=0)
    grad_normed_one = scatter_weight(
        lambda step: lax.dynamic_slice_in_dim(
            grad_normed_local, ((place + step) % groups) * quarter, quarter, 0
        ),
    )
    scale_rows = lax.dynamic_slice_in_dim(scale_one, first_row, quarter, 0)
    weighted_one = grad_normed_one * norm_one
    input_result = (
        grad_second
        + scale_rows * weighted_one
        - input_rows * scale_rows**3 * jnp.mean(input_rows * weighted_one, axis=-1, keepdims=True)
    )

    router_cols = EXPERTS // groups
    logits_mine = lax.dynamic_slice_in_dim(second_all, D + place * router_cols, router_cols, 1)
    tokens_turned = lax.dynamic_slice_in_dim(
        jnp.concatenate([logits_mine, logits_mine], axis=0), first_row, length, 0
    )
    router_part = lax.dot_general(
        tokens_turned, tokens_own[:, :D], (((0,), (0,)), ((), ())), preferred_element_type=F32
    )
    rows = D // owners
    gain_width = HD // owners
    gains = jnp.concatenate([query_gain_part, key_gain_part]).reshape(2 * head_count, owners, gain_width)
    gains = jnp.pad(gains, ((0, 0), (0, 0), (0, rows - gain_width))).reshape(2 * head_count, D)
    small = jnp.concatenate([router_part, norm_one_part[None], norm_two_part[None], gains], axis=0)
    small = jnp.pad(small, ((0, TAIL - small.shape[0]), (0, 0))).astype(BF)
    groups = [(normed_one, [grad_query_pre, grad_key_pre, grad_values_b]), (second_all, [attended])]
    sums = dense_grads(owner, groups, small)
    reduced = scatter_expert(sums)
    tail = reduced[rows:, :rows]
    norm_one_result = sum_weight_small(tail[router_cols])
    gain_result = tail[router_cols + 2 : router_cols + 2 + 2 * head_count, :gain_width]
    width = local_width
    return (
        block_output,
        input_result,
        norm_one_result,
        reduced[:rows, :width],
        reduced[:rows, width : 2 * width],
        reduced[:rows, 2 * width : 3 * width],
        gain_result[:head_count],
        gain_result[head_count:],
        reduced[:rows, 3 * width :].T,
        tail[router_cols + 1],
        tail[:router_cols].T,
        gate_result,
        up_result,
        down_result,
    )


def solution(mesh):
    rows = P(EX, None)
    columns = P(None, WE)
    heads = P(WE, None)
    mixed = P(EX, None, WE)
    down = P(EX, WE, None)
    in_specs = (
        (rows, rows, P(), columns, columns, columns, heads, heads, heads)
        + (P(), P(), mixed, mixed, down, rows, rows, rows)
    )
    square = P(EX, WE)
    turned = P(WE, EX)
    out_specs = (
        (square, P((EX, WE), None), P(EX), square, square, square)
        + (turned, turned, turned, P(EX), square, mixed, mixed, down)
    )
    return jax.shard_map(layer, mesh=mesh, in_specs=in_specs, out_specs=out_specs, check_vma=False)
```
